128 devices in a mesh: dp: 2 (over core), lat: 8 (over z, y_hi), lon: 8 (over y_lo, x).
Axes of the slice: x: 4, y: 4 (y_hi: 2, y_lo: 2; y = y_hi * 2 + y_lo), z: 4, core: 2. Of those that a mesh axis runs over, the one named last changes fastest.
Arguments:
- fields: bfloat16 [2, 640, 1024, 128], P('dp', 'lat', 'lon'), may hold values from -6 to 6
- down_weight: bfloat16 [3, 3, 128, 128], P(None, None, 'dp'), may hold values from -0.1875 to 0.1875
- mid_weight: bfloat16 [3, 3, 128, 128], P(None, None, 'dp'), may hold values from -0.1875 to 0.1875
- up_weight: bfloat16 [3, 3, 128, 128], P(None, None, 'dp'), may hold values from -0.1875 to 0.1875
- cotangent: bfloat16 [2, 640, 1024, 128], P('dp', 'lat', 'lon'), may hold values from -6 to 6
Outputs:
- level_out: bfloat16 [2, 640, 1024, 128], P('dp', 'lat', 'lon')
- grad_fields: bfloat16 [2, 640, 1024, 128], P('dp', 'lat', 'lon')
- grad_down: float32 [3, 3, 128, 128], P(None, None, 'dp')
- grad_mid: float32 [3, 3, 128, 128], P(None, None, 'dp')
- grad_up: float32 [3, 3, 128, 128], P(None, None, 'dp')
The draws below stay inside these ranges and needn't reach their ends.
All inputs are finite; a program needn't handle non-finite values.
Results may differ from the reference program's by a relative error of at most 0.012.
Values may be sent and summed in bfloat16 or wider, within the bound.
No kernel may reach another device: no remote copies, remote signals or barrier semaphores. Data moves between devices by JAX's collectives and lax.ppermute only.
A program may use at most 128 MiB of HBM per device.

```python
import math
import jax
import jax.numpy as jnp
from jax import lax

CHANNELS = 128
MEMBERS = 2
GRID_LAT = 640
GRID_LON = 1024


def level_of(own_key, extent, split, least, largest):
    loudness = 1.0
    for axis_at, blocks in split:
        heights = jax.random.uniform(jax.random.fold_in(jax.random.fold_in(own_key, 6), axis_at), (blocks,), jnp.float32, least / len(split), largest / len(split))
        loudness = loudness * jnp.repeat(jnp.exp(heights), extent[axis_at] // blocks).reshape((-1,) + (1,) * (len(extent) - 1 - axis_at))
    return loudness


def bell_draw(stream_key, shape, spread, most, cuts=(), held_as=jnp.bfloat16):
    values = jax.random.normal(stream_key, shape, jnp.float32) * spread
    if len(cuts) > 0:
        values = level_of(stream_key, shape, cuts, -0.22, 0.18) * values
    return jnp.clip(values, min=-most, max=most).astype(held_as)


def setup_inputs(seed: int = 0) -> dict:
    keys = jax.random.split(jax.random.key(seed), 6)
    fields = bell_draw(keys[0], (MEMBERS, GRID_LAT, GRID_LON, CHANNELS), 1.0, 6.0, ((0, 2), (1, 8), (2, 8)))
    down_weight = bell_draw(keys[1], (3, 3, CHANNELS, CHANNELS), (9 * CHANNELS) ** -0.5, 0.1875, ((2, 2),))
    mid_weight = bell_draw(keys[2], (3, 3, CHANNELS, CHANNELS), (9 * CHANNELS) ** -0.5, 0.1875, ((2, 2),))
    up_weight = bell_draw(keys[3], (3, 3, CHANNELS, CHANNELS), (9 * CHANNELS) ** -0.5, 0.1875, ((2, 2),))
    cotangent = bell_draw(keys[4], (MEMBERS, GRID_LAT, GRID_LON, CHANNELS), 1.0, 6.0, ((0, 2), (1, 8), (2, 8)))
    return dict(fields=fields, down_weight=down_weight, mid_weight=mid_weight, up_weight=up_weight, cotangent=cotangent)


RULE = (((1, 0),), ((0, 1), (2, 0)))

def frame(field):
    tall = jnp.pad(field, ((0, 0), (1, 1), (0, 0), (0, 0)))
    return jnp.concatenate([tall[:, :, -1:], tall, tall[:, :, :1]], axis=2)

def apply_tap(piece, kernel):
    flat = piece.reshape(-1, piece.shape[-1]).astype(jnp.float32)
    result = jnp.dot(flat, kernel.astype(jnp.float32), preferred_element_type=jnp.float32)
    return result.reshape(piece.shape[:-1] + (kernel.shape[1],))

def outer_sum(left, right):
    flat_left = left.reshape(-1, left.shape[-1]).astype(jnp.float32)
    flat_right = right.reshape(-1, right.shape[-1]).astype(jnp.float32)
    return jnp.dot(flat_left.T, flat_right, preferred_element_type=jnp.float32)

def taps_down(padded, kernel):
    half_rows = (padded.shape[1] - 2) // 2
    half_cols = (padded.shape[2] - 2) // 2
    total = 0.0
    for row in range(3):
        for col in range(3):
            piece = padded[:, row:row + 2 * half_rows:2, col:col + 2 * half_cols:2]
            total = total + apply_tap(piece, kernel[row, col])
    return total

def taps_same(padded, kernel):
    rows = padded.shape[1] - 2
    cols = padded.shape[2] - 2
    total = 0.0
    for row in range(3):
        for col in range(3):
            total = total + apply_tap(padded[:, row:row + rows, col:col + cols], kernel[row, col])
    return total

def taps_up(padded, kernel):
    rows = padded.shape[1] - 2
    cols = padded.shape[2] - 2
    phase_rows = []
    for alpha in range(2):
        phase_cols = []
        for beta in range(2):
            total = 0.0
            for row, row_off in RULE[alpha]:
                for col, col_off in RULE[beta]:
                    piece = padded[:, 1 + row_off:1 + row_off + rows, 1 + col_off:1 + col_off + cols]
                    total = total + apply_tap(piece, kernel[row, col])
            phase_cols.append(total)
        phase_rows.append(jnp.stack(phase_cols, axis=3))
    whole = jnp.stack(phase_rows, axis=2)
    return whole.reshape(whole.shape[0], 2 * rows, 2 * cols, whole.shape[-1])

def grad_down_taps(padded, grad):
    half_rows = grad.shape[1]
    half_cols = grad.shape[2]
    table = []
    for row in range(3):
        line = []
        for col in range(3):
            piece = padded[:, row:row + 2 * half_rows:2, col:col + 2 * half_cols:2]
            line.append(outer_sum(piece, grad))
        table.append(jnp.stack(line))
    return jnp.stack(table)

def grad_same_taps(padded, grad):
    rows = grad.shape[1]
    cols = grad.shape[2]
    table = []
    for row in range(3):
        line = []
        for col in range(3):
            line.append(outer_sum(padded[:, row:row + rows, col:col + cols], grad))
        table.append(jnp.stack(line))
    return jnp.stack(table)

def grad_up_taps(padded, grad):
    rows = padded.shape[1] - 2
    cols = padded.shape[2] - 2
    entries = {}
    for alpha in range(2):
        for beta in range(2):
            phase = grad[:, alpha::2, beta::2]
            for row, row_off in RULE[alpha]:
                for col, col_off in RULE[beta]:
                    piece = padded[:, 1 + row_off:1 + row_off + rows, 1 + col_off:1 + col_off + cols]
                    entries[row, col] = outer_sum(piece, phase)
    return jnp.stack([jnp.stack([entries[row, col] for col in range(3)]) for row in range(3)])

def swap_io(kernel):
    return jnp.transpose(kernel, (0, 1, 3, 2))

def one_member(pair):
    fields, cotangent, down_weight, mid_weight, up_weight = pair
    fields = fields[None]
    cotangent = cotangent[None]
    framed_in = frame(fields)
    down = taps_down(framed_in, down_weight).astype(jnp.bfloat16)
    framed_down = frame(down)
    pre = taps_same(framed_down, mid_weight)
    mid = jax.nn.silu(pre).astype(jnp.bfloat16)
    framed_mid = frame(mid)
    level_out = (fields.astype(jnp.float32) + taps_up(framed_mid, up_weight)).astype(jnp.bfloat16)
    framed_cot = frame(cotangent)
    grad_mid_map = taps_down(framed_cot, swap_io(up_weight))
    sig = jax.nn.sigmoid(pre)
    grad_pre = (grad_mid_map * sig * (1.0 + pre * (1.0 - sig))).astype(jnp.bfloat16)
    grad_down_map = taps_same(frame(grad_pre), swap_io(mid_weight)[::-1, ::-1]).astype(jnp.bfloat16)
    grad_fields = (cotangent.astype(jnp.float32) + taps_up(frame(grad_down_map), swap_io(down_weight))).astype(jnp.bfloat16)
    up_term = grad_up_taps(framed_mid, cotangent)
    mid_term = grad_same_taps(framed_down, grad_pre)
    down_term = grad_down_taps(framed_in, grad_down_map)
    return (level_out[0], grad_fields[0], down_term, mid_term, up_term)

def reference(fields, down_weight, mid_weight, up_weight, cotangent):

    def member_step(pair):
        return one_member((pair[0], pair[1], down_weight, mid_weight, up_weight))
    level_out, grad_fields, down_terms, mid_terms, up_terms = lax.map(member_step, (fields, cotangent))
    scale = 1.0 / math.sqrt(MEMBERS * GRID_LAT * GRID_LON)
    grad_down = lax.optimization_barrier(jnp.sum(down_terms, axis=0)) * scale
    grad_mid = lax.optimization_barrier(jnp.sum(mid_terms, axis=0)) * scale
    grad_up = lax.optimization_barrier(jnp.sum(up_terms, axis=0)) * scale
    return (level_out, grad_fields, grad_down, grad_mid, grad_up)
```

```python
import math

import jax
import jax.numpy as jnp
from jax import lax
from jax.sharding import PartitionSpec as P


def extended(block, sides, width, periodic):
    for axis, dim in sides:
        count = lax.axis_size(axis)
        forward = [(i, i + 1) for i in range(count - 1)]
        if periodic:
            forward.append((count - 1, 0))
        backward = [(target, source) for source, target in forward]
        low = lax.ppermute(
            lax.slice_in_dim(block, block.shape[dim] - width, None, axis=dim), axis, forward
        )
        high = lax.ppermute(lax.slice_in_dim(block, 0, width, axis=dim), axis, backward)
        block = jnp.concatenate([low, block, high], axis=dim)
    return block


def framed(field):
    tall = extended(field, (("lat", 1),), 1, False)
    return extended(tall, (("lon", 2),), 1, True)


def convolve(padded, kernel, stride, dilate, padding):
    return lax.conv_general_dilated(
        padded,
        kernel,
        (stride, stride),
        padding,
        lhs_dilation=(dilate, dilate),
        dimension_numbers=("NHWC", "HWIO", "NHWC"),
        preferred_element_type=jnp.float32,
    )


def taps_down(padded, kernel):
    return convolve(padded, kernel, 2, 1, "VALID")


def taps_same(padded, kernel):
    return convolve(padded, kernel, 1, 1, "VALID")


def taps_up(padded, kernel):
    return convolve(padded, kernel[::-1, ::-1], 1, 2, ((-1, 0), (-1, 0)))


def kernel_grad(padded, grad, dilate, layout):
    result = lax.conv_general_dilated(
        padded,
        grad,
        (1, 1),
        "VALID",
        rhs_dilation=(dilate, dilate),
        dimension_numbers=("CHWN", "IHWO", layout),
        preferred_element_type=jnp.float32,
    )
    return result[:3, :3]


def swap_io(kernel):
    return jnp.transpose(kernel, (0, 1, 3, 2))


def reduced(terms):
    bands = lax.axis_size("lat") * lax.axis_size("lon")
    rows, cols, ins, outs = terms.shape
    half = ins // lax.axis_size("dp")
    me = lax.axis_index("dp")
    own = lax.dynamic_slice_in_dim(terms, me * half, half, axis=2)
    other = lax.dynamic_slice_in_dim(terms, (1 - me) * half, half, axis=2)
    came = lax.ppermute(other.astype(jnp.bfloat16), "dp", [(0, 1), (1, 0)])
    both = (own + came.astype(jnp.float32)).astype(jnp.bfloat16)
    pieces = both.reshape(bands, -1, outs)
    pieces = lax.all_to_all(pieces, ("lat", "lon"), 0, 0, tiled=True)
    piece = jnp.sum(pieces.astype(jnp.float32), axis=0, keepdims=True).astype(jnp.bfloat16)
    whole = lax.all_to_all(
        jnp.broadcast_to(piece, pieces.shape), ("lat", "lon"), 0, 0, tiled=True
    )
    return whole.reshape(rows, cols, half, outs).astype(jnp.float32)


def body(fields, down_weight, mid_weight, up_weight, cotangent):
    kernel_down, kernel_mid, kernel_up = (
        lax.all_gather(down_weight, "dp", axis=2, tiled=True),
        lax.all_gather(mid_weight, "dp", axis=2, tiled=True),
        lax.all_gather(up_weight, "dp", axis=2, tiled=True),
    )
    cells = (
        fields.shape[0]
        * lax.axis_size("dp")
        * fields.shape[1]
        * lax.axis_size("lat")
        * fields.shape[2]
        * lax.axis_size("lon")
    )
    scale = 1.0 / math.sqrt(cells)
    framed_in = framed(fields)
    down = taps_down(framed_in, kernel_down).astype(jnp.bfloat16)
    framed_down = framed(down)
    pre = taps_same(framed_down, kernel_mid)
    mid = jax.nn.silu(pre).astype(jnp.bfloat16)
    framed_mid = framed(mid)
    level_out = (fields.astype(jnp.float32) + taps_up(framed_mid, kernel_up)).astype(jnp.bfloat16)
    framed_cot = framed(cotangent)
    up_term = kernel_grad(framed_cot, mid, 2, "HWCN") * scale
    grad_mid_map = taps_down(framed_cot, swap_io(kernel_up))
    sig = jax.nn.sigmoid(pre)
    grad_pre = (grad_mid_map * sig * (1.0 + pre * (1.0 - sig))).astype(jnp.bfloat16)
    mid_term = kernel_grad(framed_down, grad_pre, 1, "HWNC") * scale
    grad_down_map = taps_same(framed(grad_pre), swap_io(kernel_mid)[::-1, ::-1]).astype(
        jnp.bfloat16
    )
    down_term = kernel_grad(framed_in, grad_down_map, 2, "HWNC") * scale
    grad_fields = (
        cotangent.astype(jnp.float32) + taps_up(framed(grad_down_map), swap_io(kernel_down))
    ).astype(jnp.bfloat16)
    totals = reduced(jnp.concatenate([down_term, mid_term, up_term], axis=0))
    grad_down, grad_mid, grad_up = totals[0:3], totals[3:6], totals[6:9]
    return (level_out, grad_fields, grad_down, grad_mid, grad_up)


def solution(mesh):
    in_specs = (
        P("dp", "lat", "lon", None),
        P(None, None, "dp", None),
        P(None, None, "dp", None),
        P(None, None, "dp", None),
        P("dp", "lat", "lon", None),
    )
    out_specs = (
        P("dp", "lat", "lon", None),
        P("dp", "lat", "lon", None),
        P(None, None, "dp", None),
        P(None, None, "dp", None),
        P(None, None, "dp", None),
    )
    return jax.shard_map(body, mesh=mesh, in_specs=in_specs, out_specs=out_specs, check_vma=False)
```

```python
import functools
import math

import jax
import jax.numpy as jnp
from jax import lax
from jax.experimental import pallas as pl
from jax.experimental.pallas import tpu as pltpu
from jax.sharding import PartitionSpec as P

BF16 = jnp.bfloat16
F32 = jnp.float32
C = 128
FIELD_LOW, FIELD_HIGH = 5, 6
COT_LOW, COT_HIGH = 3, 4
ROWS = 5
EDGE = 16
TAPS = 32


def dot(left, right):
    return jnp.dot(left, right, preferred_element_type=F32)


def flat(value):
    return value.reshape(-1, value.shape[-1])


def split_row(stage, row, dest, pair, parity, west, west_at, east):
    wide = row.shape[0]
    stage[24 : 24 + wide, :] = row.astype(F32)
    stage[west_at : west_at + west.shape[0], :] = west.astype(F32)
    stage[24 + wide : 24 + wide + east.shape[0], :] = east.astype(F32)
    own = wide // 2 + 8
    for tap in range(3):
        upper = stage[pl.ds(23 + tap, own, stride=2), :]
        lower = stage[pl.ds(7 + tap, 8, stride=2), :]
        dest[pair, parity, :, tap * C : (tap + 1) * C] = jnp.concatenate(
            [upper, lower], axis=0
        ).astype(BF16)


def fine_taps(source, source_row, pair, parity, count):
    return flat(source[pl.ds(source_row + pair, count), parity])


def grads_kernel(
    half_rows,
    half_cols,
    bands,
    scale,
    where,
    fields,
    cot,
    low,
    high,
    west,
    east,
    w_down,
    w_mid,
    w_up_t,
    w_mid_t,
    own_out,
    other_out,
    mid_pairs,
    grad_pairs,
    field_taps,
    cot_taps,
    down_taps,
    pre_taps,
    stage,
    line,
    acc,
):
    lat = where[0]
    part = where[1]
    slots = half_cols + EDGE
    wide = half_cols + 8
    rows = 2 * half_rows

    def field_row(k, row, p, pair, parity):
        split_row(
            stage.at[k], row, field_taps, pair, parity, west[p], 16, east[p, 0:8]
        )

    def cot_row(k, row, p, pair, parity):
        split_row(
            stage.at[k],
            row,
            cot_taps,
            pair,
            parity,
            west[p, 0:COT_LOW],
            24 - COT_LOW,
            east[p, FIELD_HIGH : FIELD_HIGH + COT_HIGH],
        )

    for k in range(FIELD_LOW):
        field_row(k % 4, low[k], k, k // 2, k % 2)
    for k in range(COT_LOW):
        cot_row(k % 4, low[FIELD_LOW + k], k + 2, k // 2, k % 2)
    for k in range(FIELD_HIGH):
        p = FIELD_LOW + rows + k
        field_row(k % 4, high[k], p, p // 2, p % 2)
    for k in range(COT_HIGH):
        p = COT_LOW + rows + k
        cot_row(k % 4, high[FIELD_HIGH + k], p + 2, p // 2, p % 2)

    def own_rows(t, carry):
        for k in range(4):
            q = 4 * t + k
            field_row(k, fields[q], q + FIELD_LOW, 2 * t + (k + FIELD_LOW) // 2, (k + FIELD_LOW) % 2)
        for k in range(4):
            q = 4 * t + k
            cot_row(k, cot[q], q + FIELD_LOW, 2 * t + (k + COT_LOW) // 2, (k + COT_LOW) % 2)
        return carry

    lax.fori_loop(0, rows // 4, own_rows, 0)

    def on_grid(value, first):
        at = lat * half_rows + first + lax.broadcasted_iota(jnp.int32, value.shape, 0)
        return jnp.where((at >= 0) & (at < bands * half_rows), value, 0.0)

    def lay(value):
        line[:, 8 : 16, :] = value[:, wide:]
        line[:, 16 : 16 + wide, :] = value[:, :wide]

    def shifted(shift):
        upper = line[:, 16 + shift : 16 + shift + wide, :]
        lower = line[:, 8 + shift : 16 + shift, :]
        return jnp.concatenate([upper, lower], axis=1).astype(BF16)

    def strip(value):
        return value.reshape(ROWS, slots, C)

    def down_strip(t, carry):
        a = ROWS * t
        left = jnp.concatenate(
            [fine_taps(field_taps, a, r // 2, r % 2, ROWS) for r in range(3)], axis=1
        )
        value = on_grid(strip(dot(left, w_down[...])), a - 2)
        lay(value)
        for shift in range(3):
            down_taps[pl.ds(a, ROWS), :, shift * C : (shift + 1) * C] = shifted(shift - 1)
        return carry

    lax.fori_loop(0, half_rows // ROWS + 1, down_strip, 0)

    def pre_strip(t, carry):
        b = ROWS * t
        left = jnp.concatenate([flat(down_taps[pl.ds(b + r, ROWS)]) for r in range(3)], axis=1)
        pre = strip(dot(left, w_mid[...]))
        left = jnp.concatenate(
            [fine_taps(cot_taps, b, r // 2, r % 2, ROWS) for r in range(3)], axis=1
        )
        grad = strip(dot(left, w_up_t[...]))
        sig = jax.nn.sigmoid(pre)
        lay(on_grid(pre * sig, b - 1))
        for shift in range(2):
            mid_pairs[pl.ds(b, ROWS), :, shift * C : (shift + 1) * C] = line[
                :, 16 + shift : 16 + shift + half_cols, :
            ].astype(BF16)
        lay(on_grid(grad * sig * (1.0 + pre * (1.0 - sig)), b - 1))
        for shift in range(3):
            pre_taps[pl.ds(b, ROWS), :, shift * C : (shift + 1) * C] = shifted(shift - 1)
        return carry

    lax.fori_loop(0, half_rows // ROWS + 1, pre_strip, 0)

    def back_strip(t, carry):
        d = ROWS * t
        left = jnp.concatenate([flat(pre_taps[pl.ds(d + r, ROWS)]) for r in range(3)], axis=1)
        lay(on_grid(strip(dot(left, w_mid_t[...])), d))
        for shift in range(2):
            grad_pairs[pl.ds(d, ROWS), :, shift * C : (shift + 1) * C] = line[
                :, 16 + shift : 16 + shift + half_cols, :
            ].astype(BF16)
        return carry

    lax.fori_loop(0, half_rows // ROWS + 1, back_strip, 0)

    acc[...] = jnp.zeros_like(acc)
    step = 8

    def outer(left, right):
        return lax.dot_general(left, right, (((0,), (0,)), ((), ())), preferred_element_type=F32)

    def outer_strip(t, carry):
        i = step * t
        here = slice(0, half_cols)
        right = jnp.concatenate(
            [flat(field_taps[pl.ds(i + 2 + r // 2, step), r % 2, here]) for r in range(3)], axis=1
        )
        acc[0] += outer(flat(grad_pairs[pl.ds(i, step), :, 0:C]), right)
        right = jnp.concatenate(
            [flat(pre_taps[pl.ds(i + r, step), here]) for r in range(3)], axis=1
        )
        acc[1] += outer(flat(down_taps[pl.ds(i + 2, step), here, C : 2 * C]), right)
        right = jnp.concatenate(
            [flat(cot_taps[pl.ds(i + 1 + r // 2, step), r % 2, here]) for r in range(3)], axis=1
        )
        acc[2] += outer(flat(mid_pairs[pl.ds(i + 1, step), :, 0:C]), right)
        return carry

    lax.fori_loop(0, half_rows // step, outer_strip, 0)

    half = C // 2
    for tap in range(9):
        at = slice(tap * C, (tap + 1) * C)
        acc[0, :, at] = acc[0, :, at].T
    mine = pl.ds(pl.multiple_of(part * half, half), half)
    theirs = pl.ds(pl.multiple_of((1 - part) * half, half), half)
    for kind in range(3):
        for tap in range(9):
            held = 8 - tap if kind == 1 else tap
            at = slice(held * C, (held + 1) * C)
            own_out[kind * 9 + tap] = acc[kind, mine, at] * scale
            other_out[kind * 9 + tap] = (acc[kind, theirs, at] * scale).astype(BF16)
    for tap in range(27, TAPS):
        own_out[tap] = jnp.zeros((half, C), F32)
        other_out[tap] = jnp.zeros((half, C), BF16)


def up_kernel(mid_pairs, grad_pairs, fields, cot, u1, u2, u3, level_out, grad_fields, whole):
    first = ROWS * pl.program_id(0)
    half_cols = mid_pairs.shape[1]

    def spread(pairs, at, base, out, which):
        near = flat(pairs[pl.ds(at, ROWS)])
        far = flat(pairs[pl.ds(at + 1, ROWS)])
        odd = dot(near, u1[which])
        last = dot(far, u2[which])
        even = dot(jnp.concatenate([near[:, :C], far[:, :C]], axis=1), u3[which])
        for k in range(ROWS):
            at_k = slice(k * half_cols, (k + 1) * half_cols)
            whole[2 * k, pl.ds(0, half_cols, stride=2), :] = even[at_k, :C]
            whole[2 * k, pl.ds(1, half_cols, stride=2), :] = odd[at_k, :C]
            whole[2 * k + 1, pl.ds(0, half_cols, stride=2), :] = even[at_k, C:]
            whole[2 * k + 1, pl.ds(1, half_cols, stride=2), :] = odd[at_k, C:] + last[at_k]
        out[...] = (base[...].astype(F32) + whole[...]).astype(BF16)

    spread(mid_pairs, first + 1, fields, level_out, 0)
    spread(grad_pairs, first, cot, grad_fields, 1)


def halos(fields, cot):
    lat = lax.axis_size("lat")
    lon = lax.axis_size("lon")
    up = [(i, i + 1) for i in range(lat - 1)]
    low = lax.ppermute(
        jnp.concatenate([fields[-FIELD_LOW:], cot[-COT_LOW:]], axis=0), "lat", up
    )
    high = lax.ppermute(
        jnp.concatenate([fields[:FIELD_HIGH], cot[:COT_HIGH]], axis=0),
        "lat",
        [(j, i) for i, j in up],
    )

    def columns(at_field, at_cot):
        field = jnp.concatenate(
            [low[:FIELD_LOW, at_field], fields[:, at_field], high[:FIELD_HIGH, at_field]], axis=0
        )
        other = jnp.concatenate(
            [low[FIELD_LOW:, at_cot], cot[:, at_cot], high[FIELD_HIGH:, at_cot]], axis=0
        )
        return field, jnp.pad(other, ((2, 2), (0, 0), (0, 0)))

    field, other = columns(slice(-FIELD_LOW, None), slice(-COT_LOW, None))
    around = [(i, (i + 1) % lon) for i in range(lon)]
    west = lax.ppermute(jnp.concatenate([other, field], axis=1), "lon", around)
    field, other = columns(slice(0, FIELD_HIGH), slice(0, COT_HIGH))
    east = lax.ppermute(
        jnp.concatenate([field, other], axis=1), "lon", [(j, i) for i, j in around]
    )
    return low, high, west, east


def swap_io(kernel):
    return jnp.transpose(kernel, (0, 1, 3, 2))


def spread_weights(kernel):
    none = jnp.zeros((C, C), kernel.dtype)
    k = kernel
    u1 = jnp.block([[k[1, 2], k[2, 2]], [k[1, 0], k[2, 0]]])
    u2 = jnp.concatenate([k[0, 2], k[0, 0]], axis=0)
    u3 = jnp.block([[k[1, 1], k[2, 1]], [none, k[0, 1]]])
    return u1, u2, u3


def body(fields, down_weight, mid_weight, up_weight, cotangent):
    lats, lons, parts = (lax.axis_size(axis) for axis in ("lat", "lon", "dp"))
    _, rows, cols, _ = fields.shape
    half_rows, half_cols = rows // 2, cols // 2
    scale = 1.0 / math.sqrt(parts * rows * lats * cols * lons)
    fields, cotangent = fields[0], cotangent[0]
    part = lax.axis_index("dp")
    low, high, west, east = halos(fields, cotangent)
    weights = lax.all_gather(
        jnp.stack([down_weight, mid_weight, up_weight]), "dp", axis=3, tiled=True
    )
    down_w, mid_w, up_w = weights[0], weights[1], weights[2]
    where = jnp.stack([lax.axis_index("lat"), part]).astype(jnp.int32)

    vmem = pl.BlockSpec(memory_space=pltpu.VMEM)
    slots = half_cols + EDGE
    strips = half_rows + ROWS
    own, other, mid_pairs, grad_pairs = pl.pallas_call(
        functools.partial(grads_kernel, half_rows, half_cols, lats, scale),
        out_shape=(
            jax.ShapeDtypeStruct((TAPS, C // 2, C), F32),
            jax.ShapeDtypeStruct((TAPS, C // 2, C), BF16),
            jax.ShapeDtypeStruct((strips, half_cols, 2 * C), BF16),
            jax.ShapeDtypeStruct((strips, half_cols, 2 * C), BF16),
        ),
        in_specs=[pl.BlockSpec(memory_space=pltpu.SMEM)] + [vmem] * 10,
        out_specs=(vmem,) * 4,
        scratch_shapes=[
            pltpu.VMEM((strips + 1, 2, slots, 3 * C), BF16),
            pltpu.VMEM((strips + 1, 2, slots, 3 * C), BF16),
            pltpu.VMEM((strips + 2, slots, 3 * C), BF16),
            pltpu.VMEM((strips + 2, slots, 3 * C), BF16),
            pltpu.VMEM((4, cols + 48, C), F32),
            pltpu.VMEM((ROWS, slots + 16, C), F32),
            pltpu.VMEM((3, C, 9 * C), F32),
        ],
        compiler_params=pltpu.CompilerParams(vmem_limit_bytes=56 * 2**20),
        cost_estimate=pl.CostEstimate(
            flops=70 * 2 * half_rows * half_cols * C * C,
            transcendentals=half_rows * half_cols * C,
            bytes_accessed=8 * 2**20,
        ),
        name="grads",
    )(
        where,
        fields,
        cotangent,
        low,
        high,
        west,
        east,
        down_w.reshape(9 * C, C),
        mid_w.reshape(9 * C, C),
        swap_io(up_w).reshape(9 * C, C),
        swap_io(mid_w)[::-1, ::-1].reshape(9 * C, C),
    )

    spreads = [
        jnp.stack(pair) for pair in zip(spread_weights(up_w), spread_weights(swap_io(down_w)))
    ]
    block = pl.BlockSpec((2 * ROWS, cols, C), lambda i: (i, 0, 0))

    def held(array):
        return pl.BlockSpec(array.shape, lambda i: (0,) * array.ndim)

    level_out, grad_fields = pl.pallas_call(
        up_kernel,
        grid=(half_rows // ROWS,),
        out_shape=(jax.ShapeDtypeStruct(fields.shape, BF16),) * 2,
        in_specs=[held(mid_pairs), held(grad_pairs), block, block] + [held(u) for u in spreads],
        out_specs=(block, block),
        scratch_shapes=[pltpu.VMEM((2 * ROWS, cols, C), F32)],
        compiler_params=pltpu.CompilerParams(vmem_limit_bytes=32 * 2**20),
        cost_estimate=pl.CostEstimate(
            flops=18 * 2 * half_rows * half_cols * C * C,
            transcendentals=0,
            bytes_accessed=13 * 2**20,
        ),
        name="spread",
    )(mid_pairs, grad_pairs, fields, cotangent, *spreads)

    came = lax.ppermute(other, "dp", [(0, 1), (1, 0)])
    both = (own + came.astype(F32)).astype(BF16)
    pieces = both.reshape(lats * lons, -1, C)
    pieces = lax.all_to_all(pieces, ("lat", "lon"), 0, 0, tiled=True)
    piece = jnp.sum(pieces.astype(F32), axis=0, keepdims=True).astype(BF16)
    totals = lax.all_to_all(
        jnp.broadcast_to(piece, pieces.shape), ("lat", "lon"), 0, 0, tiled=True
    )
    totals = totals.reshape(TAPS, C // 2, C).astype(F32)
    grad_down, grad_mid, grad_up = (
        totals[9 * k : 9 * k + 9].reshape(3, 3, C // 2, C) for k in range(3)
    )
    return (level_out[None], grad_fields[None], grad_down, grad_mid, grad_up)


def solution(mesh):
    field = P("dp", "lat", "lon", None)
    weight = P(None, None, "dp", None)
    return jax.shard_map(
        body,
        mesh=mesh,
        in_specs=(field, weight, weight, weight, field),
        out_specs=(field, field, weight, weight, weight),
        check_vma=False,
    )
```

```python
import functools
import math

import jax
import jax.numpy as jnp
from jax import lax
from jax.experimental import pallas as pl
from jax.experimental.pallas import tpu as pltpu
from jax.sharding import PartitionSpec as P

BF16 = jnp.bfloat16
F32 = jnp.float32
C = 128
FIELD_LOW, FIELD_HIGH = 5, 6
COT_LOW, COT_HIGH = 3, 4
ROWS = 5
PAIRS = 4
CHUNKS = 4
EDGE = 16
TAPS = 32


def dot(left, right):
    return jnp.dot(left, right, preferred_element_type=F32)


def flat(value):
    return value.reshape(-1, value.shape[-1])


def split_row(stage, row, dest, block, place, west, *easts):
    wide = row.shape[0]
    stage[24 - west.shape[0] : 24, :] = west.astype(F32)
    stage[24 : 24 + wide, :] = row.astype(F32)
    at = 24 + wide
    for east in easts:
        stage[at : at + east.shape[0], :] = east.astype(F32)
        at += east.shape[0]
    own = wide // 2 + 8
    for tap in range(3):
        upper = stage[pl.ds(23 + tap, own, stride=2), :]
        lower = stage[pl.ds(7 + tap, 8, stride=2), :]
        dest[block, place, :, tap * C : (tap + 1) * C] = jnp.concatenate(
            [upper, lower], axis=0
        ).astype(BF16)


def joined(refs, count, first, offsets):
    return jnp.concatenate(
        [flat(refs[pl.ds(first + block, count), place]) for block, place in offsets], axis=1
    )


def grads_kernel(
    half_rows,
    half_cols,
    bands,
    scale,
    fields_hbm,
    cot_hbm,
    low_hbm,
    high_hbm,
    west_hbm,
    east_hbm,
    west_ends_hbm,
    east_ends_hbm,
    weights_hbm,
    own_out,
    other_out,
    mid_out,
    grad_out,
    fields,
    cot,
    low,
    high,
    west,
    east,
    west_ends,
    east_ends,
    weights,
    p_down,
    p_mid,
    p_up_t,
    p_mid_t,
    mid_pairs,
    grad_pairs,
    field_taps,
    cot_taps,
    down_taps,
    pre_taps,
    stage,
    line,
    acc,
    edge_sems,
    own_sems,
    weight_sem,
    out_sems,
):
    lat, part = lax.axis_index("lat"), lax.axis_index("dp")
    slots = half_cols + EDGE
    wide = half_cols + 8
    rows = 2 * half_rows
    chunk = rows // CHUNKS

    edge_copies = [
        pltpu.make_async_copy(source, dest, edge_sems.at[k])
        for k, (source, dest) in enumerate(
            [
                (low_hbm, low),
                (high_hbm, high),
                (west_hbm, west),
                (east_hbm, east),
                (west_ends_hbm, west_ends),
                (east_ends_hbm, east_ends),
            ]
        )
    ]
    own_copies = [
        pltpu.make_async_copy(
            source.at[pl.ds(n * chunk, chunk)], dest.at[pl.ds(n * chunk, chunk)], own_sems.at[k, n]
        )
        for n in range(CHUNKS)
        for k, (source, dest) in enumerate([(fields_hbm, fields), (cot_hbm, cot)])
    ]
    weight_copy = pltpu.make_async_copy(weights_hbm, weights, weight_sem)
    for copy in edge_copies + own_copies + [weight_copy]:
        copy.start()
    acc[...] = jnp.zeros_like(acc)
    for packed in (p_down, p_mid, p_up_t, p_mid_t):
        packed[...] = jnp.zeros_like(packed)
    for copy in edge_copies:
        copy.wait()

    def end_rows(rows_in, at, count, dest, p):
        for k in range(count):
            end = at + k if rows_in is low else low.shape[0] + at + k
            split_row(
                stage.at[k % 4],
                rows_in[at + k],
                dest,
                (p + k) // 4,
                (p + k) % 4,
                west_ends[end],
                east_ends[end],
            )

    end_rows(low, 0, FIELD_LOW, field_taps, 0)
    end_rows(low, FIELD_LOW, COT_LOW, cot_taps, 0)
    end_rows(high, 0, FIELD_HIGH, field_taps, FIELD_LOW + rows)
    end_rows(high, FIELD_HIGH, COT_HIGH, cot_taps, COT_LOW + rows)

    def own_rows(t, carry):
        for k in range(4):
            q, p = 4 * t + k, FIELD_LOW + k
            split_row(stage.at[k], fields[q], field_taps, t + p // 4, p % 4, west[q], east[q])
        for k in range(4):
            q, p = 4 * t + k, COT_LOW + k
            split_row(
                stage.at[k],
                cot[q],
                cot_taps,
                t + p // 4,
                p % 4,
                west[q, :COT_LOW],
                east[q, FIELD_HIGH:],
                east[rows + t, 2 * k : 2 * k + 2],
            )
        return carry

    for n in range(CHUNKS):
        own_copies[2 * n].wait()
        own_copies[2 * n + 1].wait()
        lax.fori_loop(n * chunk // 4, (n + 1) * chunk // 4, own_rows, 0)

    weight_copy.wait()
    for kind, packed, apart, swapped, turned in (
        (0, p_down, 2, False, False),
        (1, p_mid, 1, False, False),
        (2, p_up_t, 2, True, False),
        (1, p_mid_t, 1, True, True),
    ):
        for tap in range(9):
            held = (8 - tap if turned else tap) * C
            block = weights[kind, held : held + C, :]
            block = block.T if swapped else block
            for odd in range(2):
                at = (odd * apart * 3 + tap) * C
                packed[at : at + C, odd * C : (odd + 1) * C] = block

    def on_grid(value, first):
        at = lat * half_rows + first + 2 * lax.broadcasted_iota(jnp.int32, value.shape, 0)
        return jnp.where((at >= 0) & (at < bands * half_rows), value, 0.0)

    def lay(value):
        count = value.shape[0]
        line[:count, 8:16, :] = value[:, wide:]
        line[:count, 16 : 16 + wide, :] = value[:, :wide]

    def shifted(count, shift):
        upper = line[:count, 16 + shift : 16 + shift + wide, :]
        lower = line[:count, 8 + shift : 16 + shift, :]
        return jnp.concatenate([upper, lower], axis=1).astype(BF16)

    def keep_three(dest, at, odd, count, value):
        lay(value)
        for shift in range(3):
            dest[pl.ds(at, count), odd, :, shift * C : (shift + 1) * C] = shifted(count, shift - 1)

    def keep_two(dest, at, odd, count, value):
        lay(value)
        for shift in range(2):
            dest[pl.ds(at, count), odd, :, shift * C : (shift + 1) * C] = line[
                :count, 16 + shift : 16 + shift + half_cols, :
            ].astype(BF16)

    def both_rows(value, count):
        return [value[:, odd * C : (odd + 1) * C].reshape(count, slots, C) for odd in range(2)]

    near = [(q // 2, q % 2) for q in range(4)]
    fine = [(q // 4, q % 4) for q in range(5)]

    def over_pairs(total, work):
        lax.fori_loop(0, total // PAIRS, lambda t, carry: (work(PAIRS * t, PAIRS), carry)[1], 0)
        if total % PAIRS:
            work(total // PAIRS * PAIRS, total % PAIRS)

    def down_strip(m, count):
        values = both_rows(dot(joined(field_taps, count, m, fine), p_down[...]), count)
        for odd, value in enumerate(values):
            keep_three(down_taps, m, odd, count, on_grid(value, 2 * m + odd - 2))

    def pre_strip(m, count):
        pres = both_rows(dot(joined(down_taps, count, m, near), p_mid[...]), count)
        grads = both_rows(dot(joined(cot_taps, count, m, fine), p_up_t[...]), count)
        for odd in range(2):
            pre, grad, first = pres[odd], grads[odd], 2 * m + odd - 1
            sig = jax.nn.sigmoid(pre)
            keep_two(mid_pairs, m, odd, count, on_grid(pre * sig, first))
            keep_three(
                pre_taps, m, odd, count, on_grid(grad * sig * (1.0 + pre * (1.0 - sig)), first)
            )

    def back_strip(m, count):
        values = both_rows(dot(joined(pre_taps, count, m, near), p_mid_t[...]), count)
        for odd, value in enumerate(values):
            keep_two(grad_pairs, m, odd, count, on_grid(value, 2 * m + odd))

    over_pairs(half_rows // 2 + 3, down_strip)
    over_pairs(half_rows // 2 + 2, pre_strip)
    mid_copy = pltpu.make_async_copy(mid_pairs, mid_out, out_sems.at[0])
    mid_copy.start()
    over_pairs(half_rows // 2 + 1, back_strip)
    grad_copy = pltpu.make_async_copy(grad_pairs, grad_out, out_sems.at[1])
    grad_copy.start()

    here = slice(0, half_cols)

    def outer(kind, left, right):
        left = jnp.concatenate([flat(piece) for piece in left], axis=0)
        right = jnp.concatenate(
            [jnp.concatenate([flat(piece) for piece in pieces], axis=1) for pieces in right], axis=0
        )
        acc[kind] += lax.dot_general(
            left, right, (((0,), (0,)), ((), ())), preferred_element_type=F32
        )

    def outer_strip(t, carry):
        m = PAIRS * t

        def piece(ref, cells, every, row):
            return ref[pl.ds(m + row // every, PAIRS), row % every, here, cells]

        every_lane, middle, first_lane = slice(None), slice(C, 2 * C), slice(0, C)
        outer(
            0,
            [piece(grad_pairs, first_lane, 2, odd) for odd in range(2)],
            [[piece(field_taps, every_lane, 4, 4 + 2 * odd + r) for r in range(3)] for odd in range(2)],
        )
        outer(
            1,
            [piece(down_taps, middle, 2, 2 + odd) for odd in range(2)],
            [[piece(pre_taps, every_lane, 2, odd + r) for r in range(3)] for odd in range(2)],
        )
        outer(
            2,
            [piece(mid_pairs, first_lane, 2, 1 + odd) for odd in range(2)],
            [[piece(cot_taps, every_lane, 4, 2 + 2 * odd + r) for r in range(3)] for odd in range(2)],
        )
        return carry

    lax.fori_loop(0, half_rows // (2 * PAIRS), outer_strip, 0)

    half = C // 2
    for tap in range(9):
        at = slice(tap * C, (tap + 1) * C)
        acc[0, :, at] = acc[0, :, at].T
    mine = pl.ds(pl.multiple_of(part * half, half), half)
    theirs = pl.ds(pl.multiple_of((1 - part) * half, half), half)
    for kind in range(3):
        for tap in range(9):
            held = 8 - tap if kind == 1 else tap
            at = slice(held * C, (held + 1) * C)
            own_out[kind * 9 + tap] = acc[kind, mine, at] * scale
            other_out[kind * 9 + tap] = (acc[kind, theirs, at] * scale).astype(BF16)
    for tap in range(27, TAPS):
        own_out[tap] = jnp.zeros((half, C), F32)
        other_out[tap] = jnp.zeros((half, C), BF16)
    mid_copy.wait()
    grad_copy.wait()


def up_kernel(
    above,
    kind,
    swapped,
    pairs_hbm,
    base_hbm,
    weights_hbm,
    out_hbm,
    pairs,
    base,
    kernel,
    out,
    whole,
    in_sems,
    out_sems,
):
    half_cols = pairs.shape[1]
    fine = 2 * ROWS
    strips = base.shape[0] // fine
    whole_copies = [
        pltpu.make_async_copy(source, dest, in_sems.at[strips + k])
        for k, (source, dest) in enumerate([(weights_hbm.at[kind], kernel), (pairs_hbm, pairs)])
    ]

    def rows(n):
        return pl.ds(n * fine, fine)

    base_copies = [
        pltpu.make_async_copy(base_hbm.at[rows(n)], base.at[rows(n)], in_sems.at[n])
        for n in range(strips)
    ]
    out_copies = [
        pltpu.make_async_copy(out.at[rows(n)], out_hbm.at[rows(n)], out_sems.at[n])
        for n in range(strips)
    ]
    for copy in whole_copies + base_copies:
        copy.start()
    for copy in whole_copies:
        copy.wait()

    def tap(row, col):
        k = 3 * row + col
        block = kernel[k * C : (k + 1) * C, :]
        return block.T if swapped else block

    def lanes(*pieces):
        return jnp.concatenate(pieces, axis=1)

    odd_kernel = jnp.concatenate([lanes(tap(1, 2), tap(2, 2)), lanes(tap(1, 0), tap(2, 0))], axis=0)
    last_kernel = jnp.concatenate([tap(0, 2), tap(0, 0)], axis=0)
    even_kernel = jnp.concatenate(
        [lanes(tap(1, 1), tap(2, 1)), lanes(jnp.zeros((C, C), BF16), tap(0, 1))], axis=0
    )
    for n in range(strips):
        at = ROWS * n + above
        near = flat(pairs[at : at + ROWS])
        far = flat(pairs[at + 1 : at + 1 + ROWS])
        odd = dot(near, odd_kernel)
        last = dot(far, last_kernel)
        even = dot(lanes(near[:, :C], far[:, :C]), even_kernel)
        for k in range(ROWS):
            at_k = slice(k * half_cols, (k + 1) * half_cols)
            whole[2 * k, pl.ds(0, half_cols, stride=2), :] = even[at_k, :C]
            whole[2 * k, pl.ds(1, half_cols, stride=2), :] = odd[at_k, :C]
            whole[2 * k + 1, pl.ds(0, half_cols, stride=2), :] = even[at_k, C:]
            whole[2 * k + 1, pl.ds(1, half_cols, stride=2), :] = odd[at_k, C:] + last[at_k]
        base_copies[n].wait()
        out[rows(n)] = (base[rows(n)].astype(F32) + whole[...]).astype(BF16)
        out_copies[n].start()
    for copy in out_copies:
        copy.wait()


def spread(name, above, kind, swapped, pairs, base, weights):
    rows, cols, _ = base.shape
    strips = rows // (2 * ROWS)
    hbm = pl.BlockSpec(memory_space=pltpu.HBM)
    return pl.pallas_call(
        functools.partial(up_kernel, above, kind, swapped),
        out_shape=jax.ShapeDtypeStruct(base.shape, BF16),
        in_specs=[hbm] * 3,
        out_specs=hbm,
        scratch_shapes=[
            pltpu.VMEM(shape, BF16)
            for shape in (pairs.shape, base.shape, weights.shape[1:], base.shape)
        ]
        + [
            pltpu.VMEM((2 * ROWS, cols, C), F32),
            pltpu.SemaphoreType.DMA((strips + 2,)),
            pltpu.SemaphoreType.DMA((strips,)),
        ],
        compiler_params=pltpu.CompilerParams(vmem_limit_bytes=60 * 2**20),
        cost_estimate=pl.CostEstimate(
            flops=9 * rows * cols * C * C // 2, transcendentals=0, bytes_accessed=7 * 2**20
        ),
        name=name,
    )(pairs, base, weights)


def copied(name, out_shapes, moves, limit, *arrays):
    def kernel(*refs):
        ins, outs, sems = refs[: len(arrays)], refs[len(arrays) : -1], refs[-1]
        copies = [
            pltpu.make_async_copy(ins[i].at[cut], outs[o].at[place], sems.at[k])
            for k, (i, cut, o, place) in enumerate(moves)
        ]
        for copy in copies:
            copy.start()
        for copy in copies:
            copy.wait()

    return pl.pallas_call(
        kernel,
        out_shape=tuple(jax.ShapeDtypeStruct(shape, BF16) for shape in out_shapes),
        in_specs=[pl.BlockSpec(memory_space=pl.ANY)] * len(arrays),
        out_specs=(pl.BlockSpec(memory_space=pltpu.VMEM),) * len(out_shapes),
        scratch_shapes=[pltpu.SemaphoreType.DMA((len(moves),))],
        compiler_params=pltpu.CompilerParams(vmem_limit_bytes=limit * 2**20),
        name=name,
    )(*arrays)


def columns_kernel(fields_hbm, cot_hbm, east, west, ends, spare, sems):
    rows, cols, _ = fields_hbm.shape
    copies = [
        pltpu.make_async_copy(source.at[:, pl.ds(at, 8), :], ends.at[k], sems.at[k])
        for k, (source, at) in enumerate(
            [(fields_hbm, cols - 8), (cot_hbm, cols - 8), (fields_hbm, 0), (cot_hbm, 0)]
        )
    ]
    for copy in copies:
        copy.start()
    for copy in copies:
        copy.wait()
    field, other = ends[0].astype(F32), ends[1].astype(F32)
    east[...] = jnp.concatenate(
        [other[:, 8 - COT_LOW :], field[:, 8 - FIELD_LOW :]], axis=1
    ).astype(BF16)
    field, other = ends[2].astype(F32), ends[3].astype(F32)
    beside = 8 - FIELD_HIGH
    west[:rows] = jnp.concatenate([field[:, :FIELD_HIGH], other[:, :beside]], axis=1).astype(BF16)
    other = other.reshape(rows // 4, 4, 8, C)
    for k in range(4):
        spare[:, 2 * k : 2 * k + 2, :] = other[:, k, beside:COT_HIGH]
    west[rows:] = spare[...].astype(BF16)


def columns(fields, cot):
    rows = fields.shape[0]
    vmem = pl.BlockSpec(memory_space=pltpu.VMEM)
    return pl.pallas_call(
        columns_kernel,
        out_shape=(
            jax.ShapeDtypeStruct((rows, 8, C), BF16),
            jax.ShapeDtypeStruct((rows + rows // 4, 8, C), BF16),
        ),
        in_specs=[pl.BlockSpec(memory_space=pl.ANY)] * 2,
        out_specs=(vmem, vmem),
        scratch_shapes=[
            pltpu.VMEM((4, rows, 8, C), BF16),
            pltpu.VMEM((rows // 4, 8, C), F32),
            pltpu.SemaphoreType.DMA((4,)),
        ],
        compiler_params=pltpu.CompilerParams(vmem_limit_bytes=60 * 2**20),
        name="columns",
    )(fields, cot)


def halos(fields, cot, weights):
    lat = lax.axis_size("lat")
    lon = lax.axis_size("lon")
    rows, cols, _ = fields.shape
    lows, highs = FIELD_LOW + COT_LOW, FIELD_HIGH + COT_HIGH
    every = slice(None)

    def row(start, count):
        return (pl.ds(start, count), every, every)

    first, last = (every, pl.ds(0, 8), every), (every, pl.ds(cols - 8, 8), every)
    up, down = copied(
        "edges",
        [(lows, cols, C), (highs, cols, C)],
        [
            (0, row(rows - FIELD_LOW, FIELD_LOW), 0, row(0, FIELD_LOW)),
            (1, row(rows - COT_LOW, COT_LOW), 0, row(FIELD_LOW, COT_LOW)),
            (0, row(0, FIELD_HIGH), 1, row(0, FIELD_HIGH)),
            (1, row(0, COT_HIGH), 1, row(FIELD_HIGH, COT_HIGH)),
        ],
        60,
        fields,
        cot,
    )
    up, down, fields, cot = lax.optimization_barrier((up, down, fields, cot))
    east, west = columns(fields, cot)
    north = [(i, i + 1) for i in range(lat - 1)]
    south = [(j, i) for i, j in north]
    eastward = [(i, (i + 1) % lon) for i in range(lon)]
    westward = [(j, i) for i, j in eastward]
    low = lax.ppermute(up, "lat", north)
    high = lax.ppermute(down, "lat", south)
    from_west = lax.ppermute(east, "lon", eastward)
    from_east = lax.ppermute(west, "lon", westward)
    low, high, weights = lax.optimization_barrier((low, high, weights))
    east, west = copied(
        "ends",
        [(lows + highs, 8, C)] * 2,
        [
            (0, last, 0, row(0, lows)),
            (1, last, 0, row(lows, highs)),
            (0, first, 1, row(0, lows)),
            (1, first, 1, row(lows, highs)),
        ],
        2,
        low,
        high,
    )
    west_ends = lax.ppermute(east, "lon", eastward)
    east_ends = lax.ppermute(west, "lon", westward)
    return (low, high, from_west, from_east, west_ends, east_ends), weights


def body(fields, down_weight, mid_weight, up_weight, cotangent):
    lats, lons, parts = (lax.axis_size(axis) for axis in ("lat", "lon", "dp"))
    _, rows, cols, _ = fields.shape
    half_rows, half_cols = rows // 2, cols // 2
    scale = 1.0 / math.sqrt(parts * rows * lats * cols * lons)
    fields, cotangent = fields[0], cotangent[0]
    weights = lax.all_gather(
        jnp.stack([down_weight, mid_weight, up_weight]), "dp", axis=3, tiled=True
    )
    edges, weights = halos(fields, cotangent, weights)
    weights = weights.reshape(3, 9 * C, C)

    slots = half_cols + EDGE
    quads = half_rows // 2 + 5
    pairs = half_rows // 2 + 3
    hbm = pl.BlockSpec(memory_space=pl.ANY)
    inputs = (fields, cotangent, *edges, weights)
    own, other, mid_pairs, grad_pairs = pl.pallas_call(
        functools.partial(grads_kernel, half_rows, half_cols, lats, scale),
        out_shape=(
            jax.ShapeDtypeStruct((TAPS, C // 2, C), F32),
            jax.ShapeDtypeStruct((TAPS, C // 2, C), BF16),
            jax.ShapeDtypeStruct((pairs, 2, half_cols, 2 * C), BF16),
            jax.ShapeDtypeStruct((pairs, 2, half_cols, 2 * C), BF16),
        ),
        in_specs=[hbm] * len(inputs),
        out_specs=(pl.BlockSpec(memory_space=pltpu.VMEM),) * 2
        + (pl.BlockSpec(memory_space=pltpu.HBM),) * 2,
        scratch_shapes=[pltpu.VMEM(array.shape, BF16) for array in inputs]
        + [
            pltpu.VMEM((15 * C, 2 * C), BF16),
            pltpu.VMEM((12 * C, 2 * C), BF16),
            pltpu.VMEM((15 * C, 2 * C), BF16),
            pltpu.VMEM((12 * C, 2 * C), BF16),
            pltpu.VMEM((pairs, 2, half_cols, 2 * C), BF16),
            pltpu.VMEM((pairs, 2, half_cols, 2 * C), BF16),
            pltpu.VMEM((quads, 4, slots, 3 * C), BF16),
            pltpu.VMEM((quads, 4, slots, 3 * C), BF16),
            pltpu.VMEM((pairs + 1, 2, slots, 3 * C), BF16),
            pltpu.VMEM((pairs + 1, 2, slots, 3 * C), BF16),
            pltpu.VMEM((4, cols + 48, C), F32),
            pltpu.VMEM((PAIRS, slots + 16, C), F32),
            pltpu.VMEM((3, C, 9 * C), F32),
            pltpu.SemaphoreType.DMA((6,)),
            pltpu.SemaphoreType.DMA((2, CHUNKS)),
            pltpu.SemaphoreType.DMA,
            pltpu.SemaphoreType.DMA((2,)),
        ],
        compiler_params=pltpu.CompilerParams(vmem_limit_bytes=50 * 2**20),
        cost_estimate=pl.CostEstimate(
            flops=70 * 2 * half_rows * half_cols * C * C,
            transcendentals=half_rows * half_cols * C,
            bytes_accessed=8 * 2**20,
        ),
        name="grads",
    )(*inputs)
    mid_pairs = mid_pairs.reshape(2 * pairs, half_cols, 2 * C)
    grad_pairs = grad_pairs.reshape(2 * pairs, half_cols, 2 * C)

    came = lax.ppermute(other, "dp", [(0, 1), (1, 0)])
    both = (own + came.astype(F32)).astype(BF16)
    pieces = both.reshape(lats * lons, -1, C)
    pieces = lax.all_to_all(pieces, ("lat", "lon"), 0, 0, tiled=True)
    level_out = spread("level", 1, 2, False, mid_pairs, fields, weights)
    piece = jnp.sum(pieces.astype(F32), axis=0, keepdims=True).astype(BF16)
    piece, level_out = lax.optimization_barrier((piece, level_out))
    totals = lax.all_to_all(
        jnp.broadcast_to(piece, pieces.shape), ("lat", "lon"), 0, 0, tiled=True
    )
    _, grad_pairs = lax.optimization_barrier((piece, grad_pairs))
    grad_fields = spread("gradient", 0, 0, True, grad_pairs, cotangent, weights)
    totals = totals.reshape(TAPS, C // 2, C).astype(F32)
    grad_down, grad_mid, grad_up = (
        totals[9 * k : 9 * k + 9].reshape(3, 3, C // 2, C) for k in range(3)
    )
    return (level_out[None], grad_fields[None], grad_down, grad_mid, grad_up)


def solution(mesh):
    field = P("dp", "lat", "lon", None)
    weight = P(None, None, "dp", None)
    return jax.shard_map(
        body,
        mesh=mesh,
        in_specs=(field, weight, weight, weight, field),
        out_specs=(field, field, weight, weight, weight),
        check_vma=False,
    )
```

```python
import functools
import math

import jax
import jax.numpy as jnp
from jax import lax
from jax.experimental import pallas as pl
from jax.experimental.pallas import tpu as pltpu
from jax.sharding import PartitionSpec as P

BF16 = jnp.bfloat16
F32 = jnp.float32
C = 128
FIELD_LOW, FIELD_HIGH = 5, 6
COT_LOW, COT_HIGH = 3, 4
ROWS = 5
PAIRS = 4
CHUNKS = 4
EDGE = 16
LOW_ENDS, HIGH_ENDS = 2 * FIELD_LOW + 2, 2 * FIELD_HIGH + 2
TAPS = 32


def dot(left, right):
    return jnp.dot(left, right, preferred_element_type=F32)


def flat(value):
    return value.reshape(-1, value.shape[-1])


def split_row(stage, row, dest, block, place, west, *easts):
    wide = row.shape[0]
    stage[24 - west.shape[0] : 24, :] = west.astype(F32)
    stage[24 : 24 + wide, :] = row.astype(F32)
    at = 24 + wide
    for east in easts:
        stage[at : at + east.shape[0], :] = east.astype(F32)
        at += east.shape[0]
    own = wide // 2 + 8
    for tap in range(3):
        upper = stage[pl.ds(23 + tap, own, stride=2), :]
        lower = stage[pl.ds(7 + tap, 8, stride=2), :]
        dest[block, place, :, tap * C : (tap + 1) * C] = jnp.concatenate(
            [upper, lower], axis=0
        ).astype(BF16)


def joined(refs, count, first, offsets):
    return jnp.concatenate(
        [flat(refs[pl.ds(first + block, count), place]) for block, place in offsets], axis=1
    )


def grads_kernel(
    half_rows,
    half_cols,
    bands,
    scale,
    fields_hbm,
    cot_hbm,
    low_hbm,
    high_hbm,
    west_hbm,
    east_hbm,
    low_ends_hbm,
    high_ends_hbm,
    weights_hbm,
    own_out,
    other_out,
    mid_out,
    grad_out,
    fields,
    cot,
    low,
    high,
    west,
    east,
    low_ends,
    high_ends,
    weights,
    p_down,
    p_mid,
    p_up_t,
    p_mid_t,
    mid_pairs,
    grad_pairs,
    field_taps,
    cot_taps,
    down_taps,
    pre_taps,
    stage,
    line,
    acc,
    edge_sems,
    own_sems,
    weight_sem,
    out_sems,
):
    lat, part = lax.axis_index("lat"), lax.axis_index("dp")
    slots = half_cols + EDGE
    wide = half_cols + 8
    rows = 2 * half_rows
    chunk = rows // CHUNKS

    edge_copies = [
        pltpu.make_async_copy(source, dest, edge_sems.at[k])
        for k, (source, dest) in enumerate(
            [
                (low_hbm, low),
                (high_hbm, high),
                (west_hbm, west),
                (east_hbm, east),
                (low_ends_hbm, low_ends),
                (high_ends_hbm, high_ends),
            ]
        )
    ]
    own_copies = [
        pltpu.make_async_copy(
            source.at[pl.ds(n * chunk, chunk)], dest.at[pl.ds(n * chunk, chunk)], own_sems.at[k, n]
        )
        for n in range(CHUNKS)
        for k, (source, dest) in enumerate([(fields_hbm, fields), (cot_hbm, cot)])
    ]
    weight_copy = pltpu.make_async_copy(weights_hbm, weights, weight_sem)
    for copy in edge_copies + own_copies + [weight_copy]:
        copy.start()
    acc[...] = jnp.zeros_like(acc)
    for packed in (p_down, p_mid, p_up_t, p_mid_t):
        packed[...] = jnp.zeros_like(packed)
    for copy in edge_copies:
        copy.wait()

    def end_rows(rows_in, ends, fields_in, cots_in, row_of_cot, first_row, field_at, cot_at):
        for k in range(fields_in):
            split_row(
                stage.at[k % 4],
                rows_in[k],
                field_taps,
                (field_at + k) // 4,
                (field_at + k) % 4,
                ends[k],
                ends[fields_in + k],
            )
        for k in range(cots_in):
            end = row_of_cot + k
            spare = 2 * ((first_row + end) % 4)
            split_row(
                stage.at[k % 4],
                rows_in[fields_in + k],
                cot_taps,
                (cot_at + k) // 4,
                (cot_at + k) % 4,
                ends[end, :COT_LOW],
                ends[fields_in + end, FIELD_HIGH:],
                ends[2 * fields_in + (first_row % 4 + end) // 4, spare : spare + 2],
            )

    end_rows(low, low_ends, FIELD_LOW, COT_LOW, FIELD_LOW - COT_LOW, rows - FIELD_LOW, 0, 0)
    end_rows(high, high_ends, FIELD_HIGH, COT_HIGH, 0, 0, FIELD_LOW + rows, COT_LOW + rows)

    def own_rows(t, carry):
        for k in range(4):
            q, p = 4 * t + k, FIELD_LOW + k
            split_row(stage.at[k], fields[q], field_taps, t + p // 4, p % 4, west[q], east[q])
        for k in range(4):
            q, p = 4 * t + k, COT_LOW + k
            split_row(
                stage.at[k],
                cot[q],
                cot_taps,
                t + p // 4,
                p % 4,
                west[q, :COT_LOW],
                east[q, FIELD_HIGH:],
                east[rows + t, 2 * k : 2 * k + 2],
            )
        return carry

    for n in range(CHUNKS):
        own_copies[2 * n].wait()
        own_copies[2 * n + 1].wait()
        lax.fori_loop(n * chunk // 4, (n + 1) * chunk // 4, own_rows, 0)

    weight_copy.wait()
    for kind, packed, apart, swapped, turned in (
        (0, p_down, 2, False, False),
        (1, p_mid, 1, False, False),
        (2, p_up_t, 2, True, False),
        (1, p_mid_t, 1, True, True),
    ):
        for tap in range(9):
            held = (8 - tap if turned else tap) * C
            block = weights[kind, held : held + C, :]
            block = block.T if swapped else block
            for odd in range(2):
                at = (odd * apart * 3 + tap) * C
                packed[at : at + C, odd * C : (odd + 1) * C] = block

    def on_grid(value, first):
        at = lat * half_rows + first + 2 * lax.broadcasted_iota(jnp.int32, value.shape, 0)
        return jnp.where((at >= 0) & (at < bands * half_rows), value, 0.0)

    def lay(value):
        count = value.shape[0]
        line[:count, 8:16, :] = value[:, wide:]
        line[:count, 16 : 16 + wide, :] = value[:, :wide]

    def shifted(count, shift):
        upper = line[:count, 16 + shift : 16 + shift + wide, :]
        lower = line[:count, 8 + shift : 16 + shift, :]
        return jnp.concatenate([upper, lower], axis=1).astype(BF16)

    def keep_three(dest, at, odd, count, value):
        lay(value)
        for shift in range(3):
            dest[pl.ds(at, count), odd, :, shift * C : (shift + 1) * C] = shifted(count, shift - 1)

    def keep_two(dest, at, odd, count, value):
        lay(value)
        for shift in range(2):
            dest[pl.ds(at, count), odd, :, shift * C : (shift + 1) * C] = line[
                :count, 16 + shift : 16 + shift + half_cols, :
            ].astype(BF16)

    def both_rows(value, count):
        return [value[:, odd * C : (odd + 1) * C].reshape(count, slots, C) for odd in range(2)]

    near = [(q // 2, q % 2) for q in range(4)]
    fine = [(q // 4, q % 4) for q in range(5)]

    def over_pairs(total, work):
        lax.fori_loop(0, total // PAIRS, lambda t, carry: (work(PAIRS * t, PAIRS), carry)[1], 0)
        if total % PAIRS:
            work(total // PAIRS * PAIRS, total % PAIRS)

    def down_strip(m, count):
        values = both_rows(dot(joined(field_taps, count, m, fine), p_down[...]), count)
        for odd, value in enumerate(values):
            keep_three(down_taps, m, odd, count, on_grid(value, 2 * m + odd - 2))

    def pre_strip(m, count):
        pres = both_rows(dot(joined(down_taps, count, m, near), p_mid[...]), count)
        grads = both_rows(dot(joined(cot_taps, count, m, fine), p_up_t[...]), count)
        for odd in range(2):
            pre, grad, first = pres[odd], grads[odd], 2 * m + odd - 1
            sig = jax.nn.sigmoid(pre)
            keep_two(mid_pairs, m, odd, count, on_grid(pre * sig, first))
            keep_three(
                pre_taps, m, odd, count, on_grid(grad * sig * (1.0 + pre * (1.0 - sig)), first)
            )

    def back_strip(m, count):
        values = both_rows(dot(joined(pre_taps, count, m, near), p_mid_t[...]), count)
        for odd, value in enumerate(values):
            keep_two(grad_pairs, m, odd, count, on_grid(value, 2 * m + odd))

    over_pairs(half_rows // 2 + 3, down_strip)
    over_pairs(half_rows // 2 + 2, pre_strip)
    mid_copy = pltpu.make_async_copy(mid_pairs, mid_out, out_sems.at[0])
    mid_copy.start()
    over_pairs(half_rows // 2 + 1, back_strip)
    grad_copy = pltpu.make_async_copy(grad_pairs, grad_out, out_sems.at[1])
    grad_copy.start()

    here = slice(0, half_cols)

    def outer(kind, left, right):
        left = jnp.concatenate([flat(piece) for piece in left], axis=0)
        right = jnp.concatenate(
            [jnp.concatenate([flat(piece) for piece in pieces], axis=1) for pieces in right], axis=0
        )
        acc[kind] += lax.dot_general(
            left, right, (((0,), (0,)), ((), ())), preferred_element_type=F32
        )

    def outer_strip(t, carry):
        m = PAIRS * t

        def piece(ref, cells, every, row):
            return ref[pl.ds(m + row // every, PAIRS), row % every, here, cells]

        every_lane, middle, first_lane = slice(None), slice(C, 2 * C), slice(0, C)
        outer(
            0,
            [piece(grad_pairs, first_lane, 2, odd) for odd in range(2)],
            [[piece(field_taps, every_lane, 4, 4 + 2 * odd + r) for r in range(3)] for odd in range(2)],
        )
        outer(
            1,
            [piece(down_taps, middle, 2, 2 + odd) for odd in range(2)],
            [[piece(pre_taps, every_lane, 2, odd + r) for r in range(3)] for odd in range(2)],
        )
        outer(
            2,
            [piece(mid_pairs, first_lane, 2, 1 + odd) for odd in range(2)],
            [[piece(cot_taps, every_lane, 4, 2 + 2 * odd + r) for r in range(3)] for odd in range(2)],
        )
        return carry

    lax.fori_loop(0, half_rows // (2 * PAIRS), outer_strip, 0)

    half = C // 2
    for tap in range(9):
        at = slice(tap * C, (tap + 1) * C)
        acc[0, :, at] = acc[0, :, at].T
    mine = pl.ds(pl.multiple_of(part * half, half), half)
    theirs = pl.ds(pl.multiple_of((1 - part) * half, half), half)
    for kind in range(3):
        for tap in range(9):
            held = 8 - tap if kind == 1 else tap
            at = slice(held * C, (held + 1) * C)
            own_out[kind * 9 + tap] = acc[kind, mine, at] * scale
            other_out[kind * 9 + tap] = (acc[kind, theirs, at] * scale).astype(BF16)
    for tap in range(27, TAPS):
        own_out[tap] = jnp.zeros((half, C), F32)
        other_out[tap] = jnp.zeros((half, C), BF16)
    mid_copy.wait()
    grad_copy.wait()


def up_kernel(
    above,
    kind,
    swapped,
    pairs_hbm,
    base_hbm,
    weights_hbm,
    out_hbm,
    pairs,
    base,
    kernel,
    out,
    whole,
    in_sems,
    out_sems,
):
    half_cols = pairs.shape[1]
    fine = 2 * ROWS
    strips = base.shape[0] // fine
    whole_copies = [
        pltpu.make_async_copy(source, dest, in_sems.at[strips + k])
        for k, (source, dest) in enumerate([(weights_hbm.at[kind], kernel), (pairs_hbm, pairs)])
    ]

    def rows(n):
        return pl.ds(n * fine, fine)

    base_copies = [
        pltpu.make_async_copy(base_hbm.at[rows(n)], base.at[rows(n)], in_sems.at[n])
        for n in range(strips)
    ]
    out_copies = [
        pltpu.make_async_copy(out.at[rows(n)], out_hbm.at[rows(n)], out_sems.at[n])
        for n in range(strips)
    ]
    for copy in whole_copies + base_copies:
        copy.start()
    for copy in whole_copies:
        copy.wait()

    def tap(row, col):
        k = 3 * row + col
        block = kernel[k * C : (k + 1) * C, :]
        return block.T if swapped else block

    def lanes(*pieces):
        return jnp.concatenate(pieces, axis=1)

    odd_kernel = jnp.concatenate([lanes(tap(1, 2), tap(2, 2)), lanes(tap(1, 0), tap(2, 0))], axis=0)
    last_kernel = jnp.concatenate([tap(0, 2), tap(0, 0)], axis=0)
    even_kernel = jnp.concatenate(
        [lanes(tap(1, 1), tap(2, 1)), lanes(jnp.zeros((C, C), BF16), tap(0, 1))], axis=0
    )
    for n in range(strips):
        at = ROWS * n + above
        near = flat(pairs[at : at + ROWS])
        far = flat(pairs[at + 1 : at + 1 + ROWS])
        odd = dot(near, odd_kernel)
        last = dot(far, last_kernel)
        even = dot(lanes(near[:, :C], far[:, :C]), even_kernel)
        for k in range(ROWS):
            at_k = slice(k * half_cols, (k + 1) * half_cols)
            whole[2 * k, pl.ds(0, half_cols, stride=2), :] = even[at_k, :C]
            whole[2 * k, pl.ds(1, half_cols, stride=2), :] = odd[at_k, :C]
            whole[2 * k + 1, pl.ds(0, half_cols, stride=2), :] = even[at_k, C:]
            whole[2 * k + 1, pl.ds(1, half_cols, stride=2), :] = odd[at_k, C:] + last[at_k]
        base_copies[n].wait()
        out[rows(n)] = (base[rows(n)].astype(F32) + whole[...]).astype(BF16)
        out_copies[n].start()
    for copy in out_copies:
        copy.wait()


def spread(name, above, kind, swapped, pairs, base, weights):
    rows, cols, _ = base.shape
    strips = rows // (2 * ROWS)
    hbm = pl.BlockSpec(memory_space=pltpu.HBM)
    return pl.pallas_call(
        functools.partial(up_kernel, above, kind, swapped),
        out_shape=jax.ShapeDtypeStruct(base.shape, BF16),
        in_specs=[hbm] * 3,
        out_specs=hbm,
        scratch_shapes=[
            pltpu.VMEM(shape, BF16)
            for shape in (pairs.shape, base.shape, weights.shape[1:], base.shape)
        ]
        + [
            pltpu.VMEM((2 * ROWS, cols, C), F32),
            pltpu.SemaphoreType.DMA((strips + 2,)),
            pltpu.SemaphoreType.DMA((strips,)),
        ],
        compiler_params=pltpu.CompilerParams(vmem_limit_bytes=60 * 2**20),
        cost_estimate=pl.CostEstimate(
            flops=9 * rows * cols * C * C // 2, transcendentals=0, bytes_accessed=7 * 2**20
        ),
        name=name,
    )(pairs, base, weights)


def copied(name, out_shapes, moves, limit, *arrays):
    def kernel(*refs):
        ins, outs, sems = refs[: len(arrays)], refs[len(arrays) : -1], refs[-1]
        copies = [
            pltpu.make_async_copy(ins[i].at[cut], outs[o].at[place], sems.at[k])
            for k, (i, cut, o, place) in enumerate(moves)
        ]
        for copy in copies:
            copy.start()
        for copy in copies:
            copy.wait()

    return pl.pallas_call(
        kernel,
        out_shape=tuple(jax.ShapeDtypeStruct(shape, BF16) for shape in out_shapes),
        in_specs=[pl.BlockSpec(memory_space=pl.ANY)] * len(arrays),
        out_specs=(pl.BlockSpec(memory_space=pltpu.VMEM),) * len(out_shapes),
        scratch_shapes=[pltpu.SemaphoreType.DMA((len(moves),))],
        compiler_params=pltpu.CompilerParams(vmem_limit_bytes=limit * 2**20),
        name=name,
    )(*arrays)


def columns_kernel(fields_hbm, cot_hbm, east, west, ends, spare, sems):
    rows, cols, _ = fields_hbm.shape
    copies = [
        pltpu.make_async_copy(source.at[:, pl.ds(at, 8), :], ends.at[k], sems.at[k])
        for k, (source, at) in enumerate(
            [(fields_hbm, cols - 8), (cot_hbm, cols - 8), (fields_hbm, 0), (cot_hbm, 0)]
        )
    ]
    for copy in copies:
        copy.start()
    for copy in copies:
        copy.wait()
    field, other = ends[0].astype(F32), ends[1].astype(F32)
    east[...] = jnp.concatenate(
        [other[:, 8 - COT_LOW :], field[:, 8 - FIELD_LOW :]], axis=1
    ).astype(BF16)
    field, other = ends[2].astype(F32), ends[3].astype(F32)
    beside = 8 - FIELD_HIGH
    west[:rows] = jnp.concatenate([field[:, :FIELD_HIGH], other[:, :beside]], axis=1).astype(BF16)
    other = other.reshape(rows // 4, 4, 8, C)
    for k in range(4):
        spare[:, 2 * k : 2 * k + 2, :] = other[:, k, beside:COT_HIGH]
    west[rows:] = spare[...].astype(BF16)


def columns(fields, cot):
    rows = fields.shape[0]
    vmem = pl.BlockSpec(memory_space=pltpu.VMEM)
    return pl.pallas_call(
        columns_kernel,
        out_shape=(
            jax.ShapeDtypeStruct((rows, 8, C), BF16),
            jax.ShapeDtypeStruct((rows + rows // 4, 8, C), BF16),
        ),
        in_specs=[pl.BlockSpec(memory_space=pl.ANY)] * 2,
        out_specs=(vmem, vmem),
        scratch_shapes=[
            pltpu.VMEM((4, rows, 8, C), BF16),
            pltpu.VMEM((rows // 4, 8, C), F32),
            pltpu.SemaphoreType.DMA((4,)),
        ],
        compiler_params=pltpu.CompilerParams(vmem_limit_bytes=60 * 2**20),
        name="columns",
    )(fields, cot)


def halos(fields, cot, weights):
    lat = lax.axis_size("lat")
    lon = lax.axis_size("lon")
    rows, cols, _ = fields.shape
    lows, highs = FIELD_LOW + COT_LOW, FIELD_HIGH + COT_HIGH
    every = slice(None)

    def row(start, count):
        return (pl.ds(start, count), every, every)

    east, west = columns(fields, cot)
    east, west, fields, cot = lax.optimization_barrier((east, west, fields, cot))
    up, down = copied(
        "edges",
        [(lows, cols, C), (highs, cols, C)],
        [
            (0, row(rows - FIELD_LOW, FIELD_LOW), 0, row(0, FIELD_LOW)),
            (1, row(rows - COT_LOW, COT_LOW), 0, row(FIELD_LOW, COT_LOW)),
            (0, row(0, FIELD_HIGH), 1, row(0, FIELD_HIGH)),
            (1, row(0, COT_HIGH), 1, row(FIELD_HIGH, COT_HIGH)),
        ],
        60,
        fields,
        cot,
    )
    north = [(i, i + 1) for i in range(lat - 1)]
    south = [(j, i) for i, j in north]
    eastward = [(i, (i + 1) % lon) for i in range(lon)]
    westward = [(j, i) for i, j in eastward]
    from_west = lax.ppermute(east, "lon", eastward)
    from_east = lax.ppermute(west, "lon", westward)
    low = lax.ppermute(up, "lat", north)
    high = lax.ppermute(down, "lat", south)
    from_west, from_east, weights = lax.optimization_barrier((from_west, from_east, weights))
    spare = rows + (rows - FIELD_LOW) // 4
    up, down = copied(
        "corners",
        [(LOW_ENDS, 8, C), (HIGH_ENDS, 8, C)],
        [
            (0, row(rows - FIELD_LOW, FIELD_LOW), 0, row(0, FIELD_LOW)),
            (1, row(rows - FIELD_LOW, FIELD_LOW), 0, row(FIELD_LOW, FIELD_LOW)),
            (1, row(spare, 2), 0, row(2 * FIELD_LOW, 2)),
            (0, row(0, FIELD_HIGH), 1, row(0, FIELD_HIGH)),
            (1, row(0, FIELD_HIGH), 1, row(FIELD_HIGH, FIELD_HIGH)),
            (1, row(rows, 2), 1, row(2 * FIELD_HIGH, 2)),
        ],
        2,
        from_west,
        from_east,
    )
    low_ends = lax.ppermute(up, "lat", north)
    high_ends = lax.ppermute(down, "lat", south)
    return (low, high, from_west, from_east, low_ends, high_ends), weights


def body(fields, down_weight, mid_weight, up_weight, cotangent):
    lats, lons, parts = (lax.axis_size(axis) for axis in ("lat", "lon", "dp"))
    _, rows, cols, _ = fields.shape
    half_rows, half_cols = rows // 2, cols // 2
    scale = 1.0 / math.sqrt(parts * rows * lats * cols * lons)
    fields, cotangent = fields[0], cotangent[0]
    weights = lax.all_gather(
        jnp.stack([down_weight, mid_weight, up_weight]), "dp", axis=3, tiled=True
    )
    edges, weights = halos(fields, cotangent, weights)
    weights = weights.reshape(3, 9 * C, C)

    slots = half_cols + EDGE
    quads = half_rows // 2 + 5
    pairs = half_rows // 2 + 3
    hbm = pl.BlockSpec(memory_space=pl.ANY)
    inputs = (fields, cotangent, *edges, weights)
    own, other, mid_pairs, grad_pairs = pl.pallas_call(
        functools.partial(grads_kernel, half_rows, half_cols, lats, scale),
        out_shape=(
            jax.ShapeDtypeStruct((TAPS, C // 2, C), F32),
            jax.ShapeDtypeStruct((TAPS, C // 2, C), BF16),
            jax.ShapeDtypeStruct((pairs, 2, half_cols, 2 * C), BF16),
            jax.ShapeDtypeStruct((pairs, 2, half_cols, 2 * C), BF16),
        ),
        in_specs=[hbm] * len(inputs),
        out_specs=(pl.BlockSpec(memory_space=pltpu.VMEM),) * 2
        + (pl.BlockSpec(memory_space=pltpu.HBM),) * 2,
        scratch_shapes=[pltpu.VMEM(array.shape, BF16) for array in inputs]
        + [
            pltpu.VMEM((15 * C, 2 * C), BF16),
            pltpu.VMEM((12 * C, 2 * C), BF16),
            pltpu.VMEM((15 * C, 2 * C), BF16),
            pltpu.VMEM((12 * C, 2 * C), BF16),
            pltpu.VMEM((pairs, 2, half_cols, 2 * C), BF16),
            pltpu.VMEM((pairs, 2, half_cols, 2 * C), BF16),
            pltpu.VMEM((quads, 4, slots, 3 * C), BF16),
            pltpu.VMEM((quads, 4, slots, 3 * C), BF16),
            pltpu.VMEM((pairs + 1, 2, slots, 3 * C), BF16),
            pltpu.VMEM((pairs + 1, 2, slots, 3 * C), BF16),
            pltpu.VMEM((4, cols + 48, C), F32),
            pltpu.VMEM((PAIRS, slots + 16, C), F32),
            pltpu.VMEM((3, C, 9 * C), F32),
            pltpu.SemaphoreType.DMA((6,)),
            pltpu.SemaphoreType.DMA((2, CHUNKS)),
            pltpu.SemaphoreType.DMA,
            pltpu.SemaphoreType.DMA((2,)),
        ],
        compiler_params=pltpu.CompilerParams(vmem_limit_bytes=50 * 2**20),
        cost_estimate=pl.CostEstimate(
            flops=70 * 2 * half_rows * half_cols * C * C,
            transcendentals=half_rows * half_cols * C,
            bytes_accessed=8 * 2**20,
        ),
        name="grads",
    )(*inputs)
    mid_pairs = mid_pairs.reshape(2 * pairs, half_cols, 2 * C)
    grad_pairs = grad_pairs.reshape(2 * pairs, half_cols, 2 * C)

    came = lax.ppermute(other, "dp", [(0, 1), (1, 0)])
    both = (own + came.astype(F32)).astype(BF16)
    pieces = both.reshape(lats * lons, -1, C)
    pieces = lax.all_to_all(pieces, ("lat", "lon"), 0, 0, tiled=True)
    level_out = spread("level", 1, 2, False, mid_pairs, fields, weights)
    piece = jnp.sum(pieces.astype(F32), axis=0, keepdims=True).astype(BF16)
    piece, level_out = lax.optimization_barrier((piece, level_out))
    totals = lax.all_to_all(
        jnp.broadcast_to(piece, pieces.shape), ("lat", "lon"), 0, 0, tiled=True
    )
    _, grad_pairs = lax.optimization_barrier((piece, grad_pairs))
    grad_fields = spread("gradient", 0, 0, True, grad_pairs, cotangent, weights)
    totals = totals.reshape(TAPS, C // 2, C).astype(F32)
    grad_down, grad_mid, grad_up = (
        totals[9 * k : 9 * k + 9].reshape(3, 3, C // 2, C) for k in range(3)
    )
    return (level_out[None], grad_fields[None], grad_down, grad_mid, grad_up)


def solution(mesh):
    field = P("dp", "lat", "lon", None)
    weight = P(None, None, "dp", None)
    return jax.shard_map(
        body,
        mesh=mesh,
        in_specs=(field, weight, weight, weight, field),
        out_specs=(field, field, weight, weight, weight),
        check_vma=False,
    )
```

```python
import functools
import math

import jax
import jax.numpy as jnp
from jax import lax
from jax.experimental import pallas as pl
from jax.experimental.pallas import tpu as pltpu
from jax.sharding import PartitionSpec as P

BF16 = jnp.bfloat16
F32 = jnp.float32
C = 128
FIELD_LOW, FIELD_HIGH = 5, 6
COT_LOW, COT_HIGH = 3, 4
ROWS = 5
PAIRS = 4
CHUNKS = 4
EDGE = 16
LOW_ENDS, HIGH_ENDS = 2 * FIELD_LOW + 2, 2 * FIELD_HIGH + 2
TAPS = 32


def dot(left, right):
    return jnp.dot(left, right, preferred_element_type=F32)


def flat(value):
    return value.reshape(-1, value.shape[-1])


def split_row(stage, row, dest, block, place, west, *easts):
    wide = row.shape[0]
    stage[24 - west.shape[0] : 24, :] = west.astype(F32)
    stage[24 : 24 + wide, :] = row.astype(F32)
    at = 24 + wide
    for east in easts:
        stage[at : at + east.shape[0], :] = east.astype(F32)
        at += east.shape[0]
    own = wide // 2 + 8
    for tap in range(3):
        upper = stage[pl.ds(23 + tap, own, stride=2), :]
        lower = stage[pl.ds(7 + tap, 8, stride=2), :]
        dest[block, place, :, tap * C : (tap + 1) * C] = jnp.concatenate(
            [upper, lower], axis=0
        ).astype(BF16)


def joined(refs, count, first, offsets):
    return jnp.concatenate(
        [flat(refs[pl.ds(first + block, count), place]) for block, place in offsets], axis=1
    )


def grads_kernel(
    half_rows,
    half_cols,
    bands,
    scale,
    fields_hbm,
    cot_hbm,
    low_hbm,
    high_hbm,
    west_hbm,
    east_hbm,
    low_ends_hbm,
    high_ends_hbm,
    weights_hbm,
    own_out,
    other_out,
    mid_out,
    grad_out,
    fields,
    cot,
    low,
    high,
    west,
    east,
    low_ends,
    high_ends,
    weights,
    p_down,
    p_mid,
    p_up_t,
    p_mid_t,
    mid_pairs,
    grad_pairs,
    field_taps,
    cot_taps,
    down_taps,
    pre_taps,
    stage,
    line,
    acc,
    edge_sems,
    own_sems,
    weight_sem,
    out_sems,
):
    lat, part = lax.axis_index("lat"), lax.axis_index("dp")
    slots = half_cols + EDGE
    wide = half_cols + 8
    rows = 2 * half_rows
    chunk = rows // CHUNKS

    edge_copies = [
        pltpu.make_async_copy(source, dest, edge_sems.at[k])
        for k, (source, dest) in enumerate(
            [
                (low_hbm, low),
                (high_hbm, high),
                (west_hbm, west),
                (east_hbm, east),
                (low_ends_hbm, low_ends),
                (high_ends_hbm, high_ends),
            ]
        )
    ]
    own_copies = [
        pltpu.make_async_copy(
            source.at[pl.ds(n * chunk, chunk)], dest.at[pl.ds(n * chunk, chunk)], own_sems.at[k, n]
        )
        for n in range(CHUNKS)
        for k, (source, dest) in enumerate([(fields_hbm, fields), (cot_hbm, cot)])
    ]
    weight_copy = pltpu.make_async_copy(weights_hbm, weights, weight_sem)
    for copy in edge_copies + own_copies + [weight_copy]:
        copy.start()
    acc[...] = jnp.zeros_like(acc)
    for packed in (p_down, p_mid, p_up_t, p_mid_t):
        packed[...] = jnp.zeros_like(packed)
    for copy in edge_copies:
        copy.wait()

    def end_rows(rows_in, ends, fields_in, cots_in, row_of_cot, first_row, field_at, cot_at):
        for k in range(fields_in):
            split_row(
                stage.at[k % 4],
                rows_in[k],
                field_taps,
                (field_at + k) // 4,
                (field_at + k) % 4,
                ends[k],
                ends[fields_in + k],
            )
        for k in range(cots_in):
            end = row_of_cot + k
            spare = 2 * ((first_row + end) % 4)
            split_row(
                stage.at[k % 4],
                rows_in[fields_in + k],
                cot_taps,
                (cot_at + k) // 4,
                (cot_at + k) % 4,
                ends[end, :COT_LOW],
                ends[fields_in + end, FIELD_HIGH:],
                ends[2 * fields_in + (first_row % 4 + end) // 4, spare : spare + 2],
            )

    end_rows(low, low_ends, FIELD_LOW, COT_LOW, FIELD_LOW - COT_LOW, rows - FIELD_LOW, 0, 0)
    end_rows(high, high_ends, FIELD_HIGH, COT_HIGH, 0, 0, FIELD_LOW + rows, COT_LOW + rows)

    def own_rows(t, carry):
        for k in range(4):
            q, p = 4 * t + k, FIELD_LOW + k
            split_row(stage.at[k], fields[q], field_taps, t + p // 4, p % 4, west[q], east[q])
        for k in range(4):
            q, p = 4 * t + k, COT_LOW + k
            split_row(
                stage.at[k],
                cot[q],
                cot_taps,
                t + p // 4,
                p % 4,
                west[q, :COT_LOW],
                east[q, FIELD_HIGH:],
                east[rows + t, 2 * k : 2 * k + 2],
            )
        return carry

    for n in range(CHUNKS):
        own_copies[2 * n].wait()
        own_copies[2 * n + 1].wait()
        lax.fori_loop(n * chunk // 4, (n + 1) * chunk // 4, own_rows, 0)

    weight_copy.wait()
    for kind, packed, apart, swapped, turned in (
        (0, p_down, 2, False, False),
        (1, p_mid, 1, False, False),
        (2, p_up_t, 2, True, False),
        (1, p_mid_t, 1, True, True),
    ):
        for tap in range(9):
            held = (8 - tap if turned else tap) * C
            block = weights[kind, held : held + C, :]
            block = block.T if swapped else block
            for odd in range(2):
                at = (odd * apart * 3 + tap) * C
                packed[at : at + C, odd * C : (odd + 1) * C] = block

    def on_grid(value, first):
        at = lat * half_rows + first + 2 * lax.broadcasted_iota(jnp.int32, value.shape, 0)
        return jnp.where((at >= 0) & (at < bands * half_rows), value, 0.0)

    def lay(value):
        count = value.shape[0]
        line[:count, 8:16, :] = value[:, wide:]
        line[:count, 16 : 16 + wide, :] = value[:, :wide]

    def shifted(count, shift):
        upper = line[:count, 16 + shift : 16 + shift + wide, :]
        lower = line[:count, 8 + shift : 16 + shift, :]
        return jnp.concatenate([upper, lower], axis=1).astype(BF16)

    def keep_three(dest, at, odd, count, value):
        lay(value)
        for shift in range(3):
            dest[pl.ds(at, count), odd, :, shift * C : (shift + 1) * C] = shifted(count, shift - 1)

    def keep_two(dest, at, odd, count, value):
        lay(value)
        for shift in range(2):
            dest[pl.ds(at, count), odd, :, shift * C : (shift + 1) * C] = line[
                :count, 16 + shift : 16 + shift + half_cols, :
            ].astype(BF16)

    def both_rows(value, count):
        return [value[:, odd * C : (odd + 1) * C].reshape(count, slots, C) for odd in range(2)]

    near = [(q // 2, q % 2) for q in range(4)]
    fine = [(q // 4, q % 4) for q in range(5)]

    def over_pairs(total, work):
        lax.fori_loop(0, total // PAIRS, lambda t, carry: (work(PAIRS * t, PAIRS), carry)[1], 0)
        if total % PAIRS:
            work(total // PAIRS * PAIRS, total % PAIRS)

    def down_strip(m, count):
        values = both_rows(dot(joined(field_taps, count, m, fine), p_down[...]), count)
        for odd, value in enumerate(values):
            keep_three(down_taps, m, odd, count, on_grid(value, 2 * m + odd - 2))

    def pre_strip(m, count):
        pres = both_rows(dot(joined(down_taps, count, m, near), p_mid[...]), count)
        grads = both_rows(dot(joined(cot_taps, count, m, fine), p_up_t[...]), count)
        for odd in range(2):
            pre, grad, first = pres[odd], grads[odd], 2 * m + odd - 1
            sig = jax.nn.sigmoid(pre)
            keep_two(mid_pairs, m, odd, count, on_grid(pre * sig, first))
            keep_three(
                pre_taps, m, odd, count, on_grid(grad * sig * (1.0 + pre * (1.0 - sig)), first)
            )

    def back_strip(m, count):
        values = both_rows(dot(joined(pre_taps, count, m, near), p_mid_t[...]), count)
        for odd, value in enumerate(values):
            keep_two(grad_pairs, m, odd, count, on_grid(value, 2 * m + odd))

    over_pairs(half_rows // 2 + 3, down_strip)
    over_pairs(half_rows // 2 + 2, pre_strip)
    mid_copy = pltpu.make_async_copy(mid_pairs, mid_out, out_sems.at[0])
    mid_copy.start()
    over_pairs(half_rows // 2 + 1, back_strip)
    grad_copy = pltpu.make_async_copy(grad_pairs, grad_out, out_sems.at[1])
    grad_copy.start()

    here = slice(0, half_cols)

    def outer(kind, left, right):
        left = jnp.concatenate([flat(piece) for piece in left], axis=0)
        right = jnp.concatenate(
            [jnp.concatenate([flat(piece) for piece in pieces], axis=1) for pieces in right], axis=0
        )
        acc[kind] += lax.dot_general(
            left, right, (((0,), (0,)), ((), ())), preferred_element_type=F32
        )

    def outer_strip(t, carry):
        m = PAIRS * t

        def piece(ref, cells, every, row):
            return ref[pl.ds(m + row // every, PAIRS), row % every, here, cells]

        every_lane, middle, first_lane = slice(None), slice(C, 2 * C), slice(0, C)
        outer(
            0,
            [piece(grad_pairs, first_lane, 2, odd) for odd in range(2)],
            [[piece(field_taps, every_lane, 4, 4 + 2 * odd + r) for r in range(3)] for odd in range(2)],
        )
        outer(
            1,
            [piece(down_taps, middle, 2, 2 + odd) for odd in range(2)],
            [[piece(pre_taps, every_lane, 2, odd + r) for r in range(3)] for odd in range(2)],
        )
        outer(
            2,
            [piece(mid_pairs, first_lane, 2, 1 + odd) for odd in range(2)],
            [[piece(cot_taps, every_lane, 4, 2 + 2 * odd + r) for r in range(3)] for odd in range(2)],
        )
        return carry

    lax.fori_loop(0, half_rows // (2 * PAIRS), outer_strip, 0)

    half = C // 2
    for tap in range(9):
        at = slice(tap * C, (tap + 1) * C)
        acc[0, :, at] = acc[0, :, at].T
    mine = pl.ds(pl.multiple_of(part * half, half), half)
    theirs = pl.ds(pl.multiple_of((1 - part) * half, half), half)
    for kind in range(3):
        for tap in range(9):
            held = 8 - tap if kind == 1 else tap
            at = slice(held * C, (held + 1) * C)
            own_out[kind * 9 + tap] = acc[kind, mine, at] * scale
            other_out[kind * 9 + tap] = (acc[kind, theirs, at] * scale).astype(BF16)
    for tap in range(27, TAPS):
        own_out[tap] = jnp.zeros((half, C), F32)
        other_out[tap] = jnp.zeros((half, C), BF16)
    mid_copy.wait()
    grad_copy.wait()


def up_kernel(
    above,
    kind,
    swapped,
    pairs_hbm,
    base_hbm,
    weights_hbm,
    out_hbm,
    pairs,
    base,
    kernel,
    out,
    whole,
    in_sems,
    out_sems,
):
    half_cols = pairs.shape[1]
    fine = 2 * ROWS
    strips = base.shape[0] // fine
    whole_copies = [
        pltpu.make_async_copy(source, dest, in_sems.at[strips + k])
        for k, (source, dest) in enumerate([(weights_hbm.at[kind], kernel), (pairs_hbm, pairs)])
    ]

    def rows(n):
        return pl.ds(n * fine, fine)

    base_copies = [
        pltpu.make_async_copy(base_hbm.at[rows(n)], base.at[rows(n)], in_sems.at[n])
        for n in range(strips)
    ]
    out_copies = [
        pltpu.make_async_copy(out.at[rows(n)], out_hbm.at[rows(n)], out_sems.at[n])
        for n in range(strips)
    ]
    for copy in whole_copies + base_copies:
        copy.start()
    for copy in whole_copies:
        copy.wait()

    def tap(row, col):
        k = 3 * row + col
        block = kernel[k * C : (k + 1) * C, :]
        return block.T if swapped else block

    def lanes(*pieces):
        return jnp.concatenate(pieces, axis=1)

    odd_kernel = jnp.concatenate([lanes(tap(1, 2), tap(2, 2)), lanes(tap(1, 0), tap(2, 0))], axis=0)
    last_kernel = jnp.concatenate([tap(0, 2), tap(0, 0)], axis=0)
    even_kernel = jnp.concatenate(
        [lanes(tap(1, 1), tap(2, 1)), lanes(jnp.zeros((C, C), BF16), tap(0, 1))], axis=0
    )
    for n in range(strips):
        at = ROWS * n + above
        near = flat(pairs[at : at + ROWS])
        far = flat(pairs[at + 1 : at + 1 + ROWS])
        odd = dot(near, odd_kernel)
        last = dot(far, last_kernel)
        even = dot(lanes(near[:, :C], far[:, :C]), even_kernel)
        for k in range(ROWS):
            at_k = slice(k * half_cols, (k + 1) * half_cols)
            whole[2 * k, pl.ds(0, half_cols, stride=2), :] = even[at_k, :C]
            whole[2 * k, pl.ds(1, half_cols, stride=2), :] = odd[at_k, :C]
            whole[2 * k + 1, pl.ds(0, half_cols, stride=2), :] = even[at_k, C:]
            whole[2 * k + 1, pl.ds(1, half_cols, stride=2), :] = odd[at_k, C:] + last[at_k]
        base_copies[n].wait()
        out[rows(n)] = (base[rows(n)].astype(F32) + whole[...]).astype(BF16)
        out_copies[n].start()
    for copy in out_copies:
        copy.wait()


def spread(name, above, kind, swapped, pairs, base, weights):
    rows, cols, _ = base.shape
    strips = rows // (2 * ROWS)
    hbm = pl.BlockSpec(memory_space=pltpu.HBM)
    return pl.pallas_call(
        functools.partial(up_kernel, above, kind, swapped),
        out_shape=jax.ShapeDtypeStruct(base.shape, BF16),
        in_specs=[hbm] * 3,
        out_specs=hbm,
        scratch_shapes=[
            pltpu.VMEM(shape, BF16)
            for shape in (pairs.shape, base.shape, weights.shape[1:], base.shape)
        ]
        + [
            pltpu.VMEM((2 * ROWS, cols, C), F32),
            pltpu.SemaphoreType.DMA((strips + 2,)),
            pltpu.SemaphoreType.DMA((strips,)),
        ],
        compiler_params=pltpu.CompilerParams(vmem_limit_bytes=60 * 2**20),
        cost_estimate=pl.CostEstimate(
            flops=9 * rows * cols * C * C // 2, transcendentals=0, bytes_accessed=7 * 2**20
        ),
        name=name,
    )(pairs, base, weights)


def copied(name, out_shapes, moves, limit, *arrays):
    def kernel(*refs):
        ins, outs, sems = refs[: len(arrays)], refs[len(arrays) : -1], refs[-1]
        copies = [
            pltpu.make_async_copy(ins[i].at[cut], outs[o].at[place], sems.at[k])
            for k, (i, cut, o, place) in enumerate(moves)
        ]
        for copy in copies:
            copy.start()
        for copy in copies:
            copy.wait()

    return pl.pallas_call(
        kernel,
        out_shape=tuple(jax.ShapeDtypeStruct(shape, BF16) for shape in out_shapes),
        in_specs=[pl.BlockSpec(memory_space=pl.ANY)] * len(arrays),
        out_specs=(pl.BlockSpec(memory_space=pltpu.VMEM),) * len(out_shapes),
        scratch_shapes=[pltpu.SemaphoreType.DMA((len(moves),))],
        compiler_params=pltpu.CompilerParams(vmem_limit_bytes=limit * 2**20),
        name=name,
    )(*arrays)


def pack_kernel(fields_hbm, cot_hbm, east, west, up, down, ends, spare, sems):
    rows, cols, _ = fields_hbm.shape
    column_copies = [
        pltpu.make_async_copy(source.at[:, pl.ds(at, 8), :], ends.at[k], sems.at[k])
        for k, (source, at) in enumerate(
            [(fields_hbm, cols - 8), (cot_hbm, cols - 8), (fields_hbm, 0), (cot_hbm, 0)]
        )
    ]
    row_copies = [
        pltpu.make_async_copy(
            source.at[pl.ds(at, count)], dest.at[pl.ds(place, count)], sems.at[4 + k]
        )
        for k, (source, at, count, dest, place) in enumerate(
            [
                (fields_hbm, rows - FIELD_LOW, FIELD_LOW, up, 0),
                (cot_hbm, rows - COT_LOW, COT_LOW, up, FIELD_LOW),
                (fields_hbm, 0, FIELD_HIGH, down, 0),
                (cot_hbm, 0, COT_HIGH, down, FIELD_HIGH),
            ]
        )
    ]
    for copy in column_copies + row_copies:
        copy.start()
    for copy in column_copies:
        copy.wait()
    field, other = ends[0].astype(F32), ends[1].astype(F32)
    east[...] = jnp.concatenate(
        [other[:, 8 - COT_LOW :], field[:, 8 - FIELD_LOW :]], axis=1
    ).astype(BF16)
    field, other = ends[2].astype(F32), ends[3].astype(F32)
    beside = 8 - FIELD_HIGH
    west[:rows] = jnp.concatenate([field[:, :FIELD_HIGH], other[:, :beside]], axis=1).astype(BF16)
    other = other.reshape(rows // 4, 4, 8, C)
    for k in range(4):
        spare[:, 2 * k : 2 * k + 2, :] = other[:, k, beside:COT_HIGH]
    west[rows:] = spare[...].astype(BF16)
    for copy in row_copies:
        copy.wait()


def packed(fields, cot):
    rows, cols, _ = fields.shape
    vmem = pl.BlockSpec(memory_space=pltpu.VMEM)
    return pl.pallas_call(
        pack_kernel,
        out_shape=(
            jax.ShapeDtypeStruct((rows, 8, C), BF16),
            jax.ShapeDtypeStruct((rows + rows // 4, 8, C), BF16),
            jax.ShapeDtypeStruct((FIELD_LOW + COT_LOW, cols, C), BF16),
            jax.ShapeDtypeStruct((FIELD_HIGH + COT_HIGH, cols, C), BF16),
        ),
        in_specs=[pl.BlockSpec(memory_space=pl.ANY)] * 2,
        out_specs=(vmem,) * 4,
        scratch_shapes=[
            pltpu.VMEM((4, rows, 8, C), BF16),
            pltpu.VMEM((rows // 4, 8, C), F32),
            pltpu.SemaphoreType.DMA((8,)),
        ],
        compiler_params=pltpu.CompilerParams(vmem_limit_bytes=52 * 2**20),
        name="pack",
    )(fields, cot)


def passed(*arrays):
    hbm = pl.BlockSpec(memory_space=pl.ANY)
    return pl.pallas_call(
        lambda *refs: None,
        out_shape=tuple(jax.ShapeDtypeStruct(array.shape, array.dtype) for array in arrays),
        in_specs=[hbm] * len(arrays),
        out_specs=(hbm,) * len(arrays),
        input_output_aliases={k: k for k in range(len(arrays))},
        compiler_params=pltpu.CompilerParams(vmem_limit_bytes=2**20),
        name="passed",
    )(*arrays)


def halos(fields, cot, weights):
    lat = lax.axis_size("lat")
    lon = lax.axis_size("lon")
    rows = fields.shape[0]
    every = slice(None)

    def row(start, count):
        return (pl.ds(start, count), every, every)

    east, west, up, down = packed(fields, cot)
    up, down = passed(up, down)
    north = [(i, i + 1) for i in range(lat - 1)]
    south = [(j, i) for i, j in north]
    eastward = [(i, (i + 1) % lon) for i in range(lon)]
    westward = [(j, i) for i, j in eastward]
    from_west = lax.ppermute(east, "lon", eastward)
    from_east = lax.ppermute(west, "lon", westward)
    low = lax.ppermute(up, "lat", north)
    high = lax.ppermute(down, "lat", south)
    spare = rows + (rows - FIELD_LOW) // 4
    up, down = copied(
        "corners",
        [(LOW_ENDS, 8, C), (HIGH_ENDS, 8, C)],
        [
            (0, row(rows - FIELD_LOW, FIELD_LOW), 0, row(0, FIELD_LOW)),
            (1, row(rows - FIELD_LOW, FIELD_LOW), 0, row(FIELD_LOW, FIELD_LOW)),
            (1, row(spare, 2), 0, row(2 * FIELD_LOW, 2)),
            (0, row(0, FIELD_HIGH), 1, row(0, FIELD_HIGH)),
            (1, row(0, FIELD_HIGH), 1, row(FIELD_HIGH, FIELD_HIGH)),
            (1, row(rows, 2), 1, row(2 * FIELD_HIGH, 2)),
        ],
        2,
        from_west,
        from_east,
    )
    up, down, weights = lax.optimization_barrier((up, down, weights))
    low_ends = lax.ppermute(up, "lat", north)
    high_ends = lax.ppermute(down, "lat", south)
    weights = lax.all_gather(weights, "dp", axis=3, tiled=True)
    return (low, high, from_west, from_east, low_ends, high_ends), weights


def body(fields, down_weight, mid_weight, up_weight, cotangent):
    lats, lons, parts = (lax.axis_size(axis) for axis in ("lat", "lon", "dp"))
    _, rows, cols, _ = fields.shape
    half_rows, half_cols = rows // 2, cols // 2
    scale = 1.0 / math.sqrt(parts * rows * lats * cols * lons)
    fields, cotangent = fields[0], cotangent[0]
    weights = jnp.stack([down_weight, mid_weight, up_weight])
    edges, weights = halos(fields, cotangent, weights)
    weights = weights.reshape(3, 9 * C, C)

    slots = half_cols + EDGE
    quads = half_rows // 2 + 5
    pairs = half_rows // 2 + 3
    hbm = pl.BlockSpec(memory_space=pl.ANY)
    inputs = (fields, cotangent, *edges, weights)
    own, other, mid_pairs, grad_pairs = pl.pallas_call(
        functools.partial(grads_kernel, half_rows, half_cols, lats, scale),
        out_shape=(
            jax.ShapeDtypeStruct((TAPS, C // 2, C), F32),
            jax.ShapeDtypeStruct((TAPS, C // 2, C), BF16),
            jax.ShapeDtypeStruct((pairs, 2, half_cols, 2 * C), BF16),
            jax.ShapeDtypeStruct((pairs, 2, half_cols, 2 * C), BF16),
        ),
        in_specs=[hbm] * len(inputs),
        out_specs=(pl.BlockSpec(memory_space=pltpu.VMEM),) * 2
        + (pl.BlockSpec(memory_space=pltpu.HBM),) * 2,
        scratch_shapes=[pltpu.VMEM(array.shape, BF16) for array in inputs]
        + [
            pltpu.VMEM((15 * C, 2 * C), BF16),
            pltpu.VMEM((12 * C, 2 * C), BF16),
            pltpu.VMEM((15 * C, 2 * C), BF16),
            pltpu.VMEM((12 * C, 2 * C), BF16),
            pltpu.VMEM((pairs, 2, half_cols, 2 * C), BF16),
            pltpu.VMEM((pairs, 2, half_cols, 2 * C), BF16),
            pltpu.VMEM((quads, 4, slots, 3 * C), BF16),
            pltpu.VMEM((quads, 4, slots, 3 * C), BF16),
            pltpu.VMEM((pairs + 1, 2, slots, 3 * C), BF16),
            pltpu.VMEM((pairs + 1, 2, slots, 3 * C), BF16),
            pltpu.VMEM((4, cols + 48, C), F32),
            pltpu.VMEM((PAIRS, slots + 16, C), F32),
            pltpu.VMEM((3, C, 9 * C), F32),
            pltpu.SemaphoreType.DMA((6,)),
            pltpu.SemaphoreType.DMA((2, CHUNKS)),
            pltpu.SemaphoreType.DMA,
            pltpu.SemaphoreType.DMA((2,)),
        ],
        compiler_params=pltpu.CompilerParams(vmem_limit_bytes=50 * 2**20),
        cost_estimate=pl.CostEstimate(
            flops=70 * 2 * half_rows * half_cols * C * C,
            transcendentals=half_rows * half_cols * C,
            bytes_accessed=8 * 2**20,
        ),
        name="grads",
    )(*inputs)
    mid_pairs = mid_pairs.reshape(2 * pairs, half_cols, 2 * C)
    grad_pairs = grad_pairs.reshape(2 * pairs, half_cols, 2 * C)

    came = lax.ppermute(other, "dp", [(0, 1), (1, 0)])
    both = (own + came.astype(F32)).astype(BF16)
    pieces = both.reshape(lats * lons, -1, C)
    pieces = lax.all_to_all(pieces, ("lat", "lon"), 0, 0, tiled=True)
    level_out = spread("level", 1, 2, False, mid_pairs, fields, weights)
    piece = jnp.sum(pieces.astype(F32), axis=0, keepdims=True).astype(BF16)
    piece, level_out = lax.optimization_barrier((piece, level_out))
    totals = lax.all_to_all(
        jnp.broadcast_to(piece, pieces.shape), ("lat", "lon"), 0, 0, tiled=True
    )
    _, grad_pairs = lax.optimization_barrier((piece, grad_pairs))
    grad_fields = spread("gradient", 0, 0, True, grad_pairs, cotangent, weights)
    totals = totals.reshape(TAPS, C // 2, C).astype(F32)
    grad_down, grad_mid, grad_up = (
        totals[9 * k : 9 * k + 9].reshape(3, 3, C // 2, C) for k in range(3)
    )
    return (level_out[None], grad_fields[None], grad_down, grad_mid, grad_up)


def solution(mesh):
    field = P("dp", "lat", "lon", None)
    weight = P(None, None, "dp", None)
    return jax.shard_map(
        body,
        mesh=mesh,
        in_specs=(field, weight, weight, weight, field),
        out_specs=(field, field, weight, weight, weight),
        check_vma=False,
    )
```

```python
import functools
import math

import jax
import jax.numpy as jnp
from jax import lax
from jax.experimental import pallas as pl
from jax.experimental.pallas import tpu as pltpu
from jax.sharding import PartitionSpec as P

BF16 = jnp.bfloat16
F32 = jnp.float32
C = 128
FIELD_LOW, FIELD_HIGH = 5, 6
COT_LOW, COT_HIGH = 3, 4
ROWS = 5
PAIRS = 12
CELL_PAIRS = 10
CHUNKS = 4
EDGE = 16
LOW_ENDS, HIGH_ENDS = 2 * FIELD_LOW + 2, 2 * FIELD_HIGH + 2
TAPS = 32


def dot(left, right):
    return jnp.dot(left, right, preferred_element_type=F32)


def flat(value):
    return value.reshape(-1, value.shape[-1])


def split_row(stage, row, dest, block, place, west, *easts):
    wide = row.shape[0]
    stage[24 - west.shape[0] : 24, :] = west.astype(F32)
    stage[24 : 24 + wide, :] = row.astype(F32)
    at = 24 + wide
    for east in easts:
        stage[at : at + east.shape[0], :] = east.astype(F32)
        at += east.shape[0]
    own = wide // 2 + 8
    for tap in range(3):
        upper = stage[pl.ds(23 + tap, own, stride=2), :]
        lower = stage[pl.ds(7 + tap, 8, stride=2), :]
        dest[block, place, :, tap * C : (tap + 1) * C] = jnp.concatenate(
            [upper, lower], axis=0
        ).astype(BF16)


def joined(refs, count, first, offsets):
    return jnp.concatenate(
        [flat(refs[pl.ds(first + block, count), place]) for block, place in offsets], axis=1
    )


def grads_kernel(
    half_rows,
    half_cols,
    bands,
    scale,
    fields_hbm,
    cot_hbm,
    low_hbm,
    high_hbm,
    west_hbm,
    east_hbm,
    low_ends_hbm,
    high_ends_hbm,
    weights_hbm,
    own_out,
    other_out,
    mid_out,
    grad_out,
    fields,
    cot,
    low,
    high,
    west,
    east,
    low_ends,
    high_ends,
    weights,
    p_down,
    p_mid,
    p_up_t,
    p_mid_t,
    mid_pairs,
    grad_pairs,
    field_taps,
    cot_taps,
    down_taps,
    pre_taps,
    stage,
    line,
    acc,
    edge_sems,
    own_sems,
    weight_sem,
    out_sems,
):
    lat, part = lax.axis_index("lat"), lax.axis_index("dp")
    slots = half_cols + EDGE
    wide = half_cols + 8
    rows = 2 * half_rows
    chunk = rows // CHUNKS

    edge_copies = [
        pltpu.make_async_copy(source, dest, edge_sems.at[k])
        for k, (source, dest) in enumerate(
            [
                (low_hbm, low),
                (high_hbm, high),
                (west_hbm, west),
                (east_hbm, east),
                (low_ends_hbm, low_ends),
                (high_ends_hbm, high_ends),
            ]
        )
    ]
    own_copies = [
        pltpu.make_async_copy(
            source.at[pl.ds(n * chunk, chunk)], dest.at[pl.ds(n * chunk, chunk)], own_sems.at[k, n]
        )
        for n in range(CHUNKS)
        for k, (source, dest) in enumerate([(fields_hbm, fields), (cot_hbm, cot)])
    ]
    weight_copy = pltpu.make_async_copy(weights_hbm, weights, weight_sem)
    for copy in edge_copies + own_copies + [weight_copy]:
        copy.start()
    acc[...] = jnp.zeros_like(acc)
    for packed in (p_down, p_mid, p_up_t, p_mid_t):
        packed[...] = jnp.zeros_like(packed)
    for copy in edge_copies:
        copy.wait()

    def end_rows(rows_in, ends, fields_in, cots_in, row_of_cot, first_row, field_at, cot_at):
        for k in range(fields_in):
            split_row(
                stage.at[k % 4],
                rows_in[k],
                field_taps,
                (field_at + k) // 4,
                (field_at + k) % 4,
                ends[k],
                ends[fields_in + k],
            )
        for k in range(cots_in):
            end = row_of_cot + k
            spare = 2 * ((first_row + end) % 4)
            split_row(
                stage.at[k % 4],
                rows_in[fields_in + k],
                cot_taps,
                (cot_at + k) // 4,
                (cot_at + k) % 4,
                ends[end, :COT_LOW],
                ends[fields_in + end, FIELD_HIGH:],
                ends[2 * fields_in + (first_row % 4 + end) // 4, spare : spare + 2],
            )

    end_rows(low, low_ends, FIELD_LOW, COT_LOW, FIELD_LOW - COT_LOW, rows - FIELD_LOW, 0, 0)
    end_rows(high, high_ends, FIELD_HIGH, COT_HIGH, 0, 0, FIELD_LOW + rows, COT_LOW + rows)

    def own_rows(t, carry):
        for k in range(4):
            q, p = 4 * t + k, FIELD_LOW + k
            split_row(stage.at[k], fields[q], field_taps, t + p // 4, p % 4, west[q], east[q])
        for k in range(4):
            q, p = 4 * t + k, COT_LOW + k
            split_row(
                stage.at[k],
                cot[q],
                cot_taps,
                t + p // 4,
                p % 4,
                west[q, :COT_LOW],
                east[q, FIELD_HIGH:],
                east[rows + t, 2 * k : 2 * k + 2],
            )
        return carry

    for n in range(CHUNKS):
        own_copies[2 * n].wait()
        own_copies[2 * n + 1].wait()
        lax.fori_loop(n * chunk // 4, (n + 1) * chunk // 4, own_rows, 0)

    weight_copy.wait()
    for kind, packed, apart, swapped, turned in (
        (0, p_down, 2, False, False),
        (1, p_mid, 1, False, False),
        (2, p_up_t, 2, True, False),
        (1, p_mid_t, 1, True, True),
    ):
        for tap in range(9):
            held = (8 - tap if turned else tap) * C
            block = weights[kind, held : held + C, :]
            block = block.T if swapped else block
            for odd in range(2):
                at = (odd * apart * 3 + tap) * C
                packed[at : at + C, odd * C : (odd + 1) * C] = block

    def on_grid(value, first):
        at = lat * half_rows + first + 2 * lax.broadcasted_iota(jnp.int32, value.shape, 0)
        return jnp.where((at >= 0) & (at < bands * half_rows), value, 0.0)

    def lay(value):
        count = value.shape[0]
        line[:count, 8:16, :] = value[:, wide:]
        line[:count, 16 : 16 + wide, :] = value[:, :wide]

    def shifted(count, shift):
        upper = line[:count, 16 + shift : 16 + shift + wide, :]
        lower = line[:count, 8 + shift : 16 + shift, :]
        return jnp.concatenate([upper, lower], axis=1).astype(BF16)

    def keep_three(dest, at, odd, count, value):
        lay(value)
        for shift in range(3):
            dest[pl.ds(at, count), odd, :, shift * C : (shift + 1) * C] = shifted(count, shift - 1)

    def keep_two(dest, at, odd, count, value):
        lay(value)
        for shift in range(2):
            dest[pl.ds(at, count), odd, :, shift * C : (shift + 1) * C] = line[
                :count, 16 + shift : 16 + shift + half_cols, :
            ].astype(BF16)

    def both_rows(value, count):
        return [value[:, odd * C : (odd + 1) * C].reshape(count, slots, C) for odd in range(2)]

    near = [(q // 2, q % 2) for q in range(4)]
    fine = [(q // 4, q % 4) for q in range(5)]

    def over_pairs(total, work):
        lax.fori_loop(0, total // PAIRS, lambda t, carry: (work(PAIRS * t, PAIRS), carry)[1], 0)
        if total % PAIRS:
            work(total // PAIRS * PAIRS, total % PAIRS)

    def down_strip(m, count):
        values = both_rows(dot(joined(field_taps, count, m, fine), p_down[...]), count)
        for odd, value in enumerate(values):
            keep_three(down_taps, m, odd, count, on_grid(value, 2 * m + odd - 2))

    def pre_strip(m, count):
        pres = both_rows(dot(joined(down_taps, count, m, near), p_mid[...]), count)
        grads = both_rows(dot(joined(cot_taps, count, m, fine), p_up_t[...]), count)
        for odd in range(2):
            pre, grad, first = pres[odd], grads[odd], 2 * m + odd - 1
            sig = jax.nn.sigmoid(pre)
            keep_two(mid_pairs, m, odd, count, on_grid(pre * sig, first))
            keep_three(
                pre_taps, m, odd, count, on_grid(grad * sig * (1.0 + pre * (1.0 - sig)), first)
            )

    def back_strip(m, count):
        values = both_rows(dot(joined(pre_taps, count, m, near), p_mid_t[...]), count)
        for odd, value in enumerate(values):
            keep_two(grad_pairs, m, odd, count, on_grid(value, 2 * m + odd))

    over_pairs(half_rows // 2 + 3, down_strip)
    over_pairs(half_rows // 2 + 2, pre_strip)
    mid_copy = pltpu.make_async_copy(mid_pairs, mid_out, out_sems.at[0])
    mid_copy.start()
    over_pairs(half_rows // 2 + 1, back_strip)
    grad_copy = pltpu.make_async_copy(grad_pairs, grad_out, out_sems.at[1])
    grad_copy.start()

    here = slice(0, half_cols)

    def outer(kind, left, right):
        left = jnp.concatenate([flat(piece) for piece in left], axis=0)
        right = jnp.concatenate(
            [jnp.concatenate([flat(piece) for piece in pieces], axis=1) for pieces in right], axis=0
        )
        acc[kind] += lax.dot_general(
            left, right, (((0,), (0,)), ((), ())), preferred_element_type=F32
        )

    def outer_strip(t, carry):
        m = CELL_PAIRS * t

        def piece(ref, cells, every, row):
            return ref[pl.ds(m + row // every, CELL_PAIRS), row % every, here, cells]

        every_lane, middle, first_lane = slice(None), slice(C, 2 * C), slice(0, C)
        outer(
            0,
            [piece(grad_pairs, first_lane, 2, odd) for odd in range(2)],
            [[piece(field_taps, every_lane, 4, 4 + 2 * odd + r) for r in range(3)] for odd in range(2)],
        )
        outer(
            1,
            [piece(down_taps, middle, 2, 2 + odd) for odd in range(2)],
            [[piece(pre_taps, every_lane, 2, odd + r) for r in range(3)] for odd in range(2)],
        )
        outer(
            2,
            [piece(mid_pairs, first_lane, 2, 1 + odd) for odd in range(2)],
            [[piece(cot_taps, every_lane, 4, 2 + 2 * odd + r) for r in range(3)] for odd in range(2)],
        )
        return carry

    lax.fori_loop(0, half_rows // (2 * CELL_PAIRS), outer_strip, 0)

    half = C // 2
    for tap in range(9):
        at = slice(tap * C, (tap + 1) * C)
        acc[0, :, at] = acc[0, :, at].T
    mine = pl.ds(pl.multiple_of(part * half, half), half)
    theirs = pl.ds(pl.multiple_of((1 - part) * half, half), half)
    for kind in range(3):
        for tap in range(9):
            held = 8 - tap if kind == 1 else tap
            at = slice(held * C, (held + 1) * C)
            own_out[kind * 9 + tap] = acc[kind, mine, at] * scale
            other_out[kind * 9 + tap] = (acc[kind, theirs, at] * scale).astype(BF16)
    for tap in range(27, TAPS):
        own_out[tap] = jnp.zeros((half, C), F32)
        other_out[tap] = jnp.zeros((half, C), BF16)
    mid_copy.wait()
    grad_copy.wait()


def up_kernel(
    above,
    kind,
    swapped,
    pairs_hbm,
    base_hbm,
    weights_hbm,
    out_hbm,
    pairs,
    base,
    kernel,
    out,
    whole,
    in_sems,
    out_sems,
):
    half_cols = pairs.shape[1]
    fine = 2 * ROWS
    strips = base.shape[0] // fine
    whole_copies = [
        pltpu.make_async_copy(source, dest, in_sems.at[strips + k])
        for k, (source, dest) in enumerate([(weights_hbm.at[kind], kernel), (pairs_hbm, pairs)])
    ]

    def rows(n):
        return pl.ds(n * fine, fine)

    base_copies = [
        pltpu.make_async_copy(base_hbm.at[rows(n)], base.at[rows(n)], in_sems.at[n])
        for n in range(strips)
    ]
    out_copies = [
        pltpu.make_async_copy(out.at[rows(n)], out_hbm.at[rows(n)], out_sems.at[n])
        for n in range(strips)
    ]
    for copy in whole_copies + base_copies:
        copy.start()
    for copy in whole_copies:
        copy.wait()

    def tap(row, col):
        k = 3 * row + col
        block = kernel[k * C : (k + 1) * C, :]
        return block.T if swapped else block

    def lanes(*pieces):
        return jnp.concatenate(pieces, axis=1)

    odd_kernel = jnp.concatenate([lanes(tap(1, 2), tap(2, 2)), lanes(tap(1, 0), tap(2, 0))], axis=0)
    last_kernel = jnp.concatenate([tap(0, 2), tap(0, 0)], axis=0)
    even_kernel = jnp.concatenate(
        [lanes(tap(1, 1), tap(2, 1)), lanes(jnp.zeros((C, C), BF16), tap(0, 1))], axis=0
    )
    for n in range(strips):
        at = ROWS * n + above
        near = flat(pairs[at : at + ROWS])
        far = flat(pairs[at + 1 : at + 1 + ROWS])
        odd = dot(near, odd_kernel)
        last = dot(far, last_kernel)
        even = dot(lanes(near[:, :C], far[:, :C]), even_kernel)
        for k in range(ROWS):
            at_k = slice(k * half_cols, (k + 1) * half_cols)
            whole[2 * k, pl.ds(0, half_cols, stride=2), :] = even[at_k, :C]
            whole[2 * k, pl.ds(1, half_cols, stride=2), :] = odd[at_k, :C]
            whole[2 * k + 1, pl.ds(0, half_cols, stride=2), :] = even[at_k, C:]
            whole[2 * k + 1, pl.ds(1, half_cols, stride=2), :] = odd[at_k, C:] + last[at_k]
        base_copies[n].wait()
        out[rows(n)] = (base[rows(n)].astype(F32) + whole[...]).astype(BF16)
        out_copies[n].start()
    for copy in out_copies:
        copy.wait()


def spread(name, above, kind, swapped, pairs, base, weights):
    rows, cols, _ = base.shape
    strips = rows // (2 * ROWS)
    hbm = pl.BlockSpec(memory_space=pltpu.HBM)
    return pl.pallas_call(
        functools.partial(up_kernel, above, kind, swapped),
        out_shape=jax.ShapeDtypeStruct(base.shape, BF16),
        in_specs=[hbm] * 3,
        out_specs=hbm,
        scratch_shapes=[
            pltpu.VMEM(shape, BF16)
            for shape in (pairs.shape, base.shape, weights.shape[1:], base.shape)
        ]
        + [
            pltpu.VMEM((2 * ROWS, cols, C), F32),
            pltpu.SemaphoreType.DMA((strips + 2,)),
            pltpu.SemaphoreType.DMA((strips,)),
        ],
        compiler_params=pltpu.CompilerParams(vmem_limit_bytes=60 * 2**20),
        cost_estimate=pl.CostEstimate(
            flops=9 * rows * cols * C * C // 2, transcendentals=0, bytes_accessed=7 * 2**20
        ),
        name=name,
    )(pairs, base, weights)


def copied(name, out_shapes, moves, limit, *arrays):
    def kernel(*refs):
        ins, outs, sems = refs[: len(arrays)], refs[len(arrays) : -1], refs[-1]
        copies = [
            pltpu.make_async_copy(ins[i].at[cut], outs[o].at[place], sems.at[k])
            for k, (i, cut, o, place) in enumerate(moves)
        ]
        for copy in copies:
            copy.start()
        for copy in copies:
            copy.wait()

    return pl.pallas_call(
        kernel,
        out_shape=tuple(jax.ShapeDtypeStruct(shape, BF16) for shape in out_shapes),
        in_specs=[pl.BlockSpec(memory_space=pl.ANY)] * len(arrays),
        out_specs=(pl.BlockSpec(memory_space=pltpu.VMEM),) * len(out_shapes),
        scratch_shapes=[pltpu.SemaphoreType.DMA((len(moves),))],
        compiler_params=pltpu.CompilerParams(vmem_limit_bytes=limit * 2**20),
        name=name,
    )(*arrays)


def pack_kernel(fields_hbm, cot_hbm, east, west, up, down, ends, spare, sems):
    rows, cols, _ = fields_hbm.shape
    column_copies = [
        pltpu.make_async_copy(source.at[:, pl.ds(at, 8), :], ends.at[k], sems.at[k])
        for k, (source, at) in enumerate(
            [(fields_hbm, cols - 8), (cot_hbm, cols - 8), (fields_hbm, 0), (cot_hbm, 0)]
        )
    ]
    row_copies = [
        pltpu.make_async_copy(
            source.at[pl.ds(at, count)], dest.at[pl.ds(place, count)], sems.at[4 + k]
        )
        for k, (source, at, count, dest, place) in enumerate(
            [
                (fields_hbm, rows - FIELD_LOW, FIELD_LOW, up, 0),
                (cot_hbm, rows - COT_LOW, COT_LOW, up, FIELD_LOW),
                (fields_hbm, 0, FIELD_HIGH, down, 0),
                (cot_hbm, 0, COT_HIGH, down, FIELD_HIGH),
            ]
        )
    ]
    for copy in column_copies + row_copies:
        copy.start()
    for copy in column_copies:
        copy.wait()
    field, other = ends[0].astype(F32), ends[1].astype(F32)
    east[...] = jnp.concatenate(
        [other[:, 8 - COT_LOW :], field[:, 8 - FIELD_LOW :]], axis=1
    ).astype(BF16)
    field, other = ends[2].astype(F32), ends[3].astype(F32)
    beside = 8 - FIELD_HIGH
    west[:rows] = jnp.concatenate([field[:, :FIELD_HIGH], other[:, :beside]], axis=1).astype(BF16)
    other = other.reshape(rows // 4, 4, 8, C)
    for k in range(4):
        spare[:, 2 * k : 2 * k + 2, :] = other[:, k, beside:COT_HIGH]
    west[rows:] = spare[...].astype(BF16)
    for copy in row_copies:
        copy.wait()


def packed(fields, cot):
    rows, cols, _ = fields.shape
    vmem = pl.BlockSpec(memory_space=pltpu.VMEM)
    return pl.pallas_call(
        pack_kernel,
        out_shape=(
            jax.ShapeDtypeStruct((rows, 8, C), BF16),
            jax.ShapeDtypeStruct((rows + rows // 4, 8, C), BF16),
            jax.ShapeDtypeStruct((FIELD_LOW + COT_LOW, cols, C), BF16),
            jax.ShapeDtypeStruct((FIELD_HIGH + COT_HIGH, cols, C), BF16),
        ),
        in_specs=[pl.BlockSpec(memory_space=pl.ANY)] * 2,
        out_specs=(vmem,) * 4,
        scratch_shapes=[
            pltpu.VMEM((4, rows, 8, C), BF16),
            pltpu.VMEM((rows // 4, 8, C), F32),
            pltpu.SemaphoreType.DMA((8,)),
        ],
        compiler_params=pltpu.CompilerParams(vmem_limit_bytes=52 * 2**20),
        name="pack",
    )(fields, cot)


def passed(*arrays):
    hbm = pl.BlockSpec(memory_space=pl.ANY)
    return pl.pallas_call(
        lambda *refs: None,
        out_shape=tuple(jax.ShapeDtypeStruct(array.shape, array.dtype) for array in arrays),
        in_specs=[hbm] * len(arrays),
        out_specs=(hbm,) * len(arrays),
        input_output_aliases={k: k for k in range(len(arrays))},
        compiler_params=pltpu.CompilerParams(vmem_limit_bytes=2**20),
        name="passed",
    )(*arrays)


def halos(fields, cot, weights):
    lat = lax.axis_size("lat")
    lon = lax.axis_size("lon")
    rows = fields.shape[0]
    every = slice(None)

    def row(start, count):
        return (pl.ds(start, count), every, every)

    east, west, up, down = packed(fields, cot)
    up, down = passed(up, down)
    north = [(i, i + 1) for i in range(lat - 1)]
    south = [(j, i) for i, j in north]
    eastward = [(i, (i + 1) % lon) for i in range(lon)]
    westward = [(j, i) for i, j in eastward]
    from_west = lax.ppermute(east, "lon", eastward)
    from_east = lax.ppermute(west, "lon", westward)
    low = lax.ppermute(up, "lat", north)
    high = lax.ppermute(down, "lat", south)
    spare = rows + (rows - FIELD_LOW) // 4
    up, down = copied(
        "corners",
        [(LOW_ENDS, 8, C), (HIGH_ENDS, 8, C)],
        [
            (0, row(rows - FIELD_LOW, FIELD_LOW), 0, row(0, FIELD_LOW)),
            (1, row(rows - FIELD_LOW, FIELD_LOW), 0, row(FIELD_LOW, FIELD_LOW)),
            (1, row(spare, 2), 0, row(2 * FIELD_LOW, 2)),
            (0, row(0, FIELD_HIGH), 1, row(0, FIELD_HIGH)),
            (1, row(0, FIELD_HIGH), 1, row(FIELD_HIGH, FIELD_HIGH)),
            (1, row(rows, 2), 1, row(2 * FIELD_HIGH, 2)),
        ],
        2,
        from_west,
        from_east,
    )
    up, down, weights = lax.optimization_barrier((up, down, weights))
    low_ends = lax.ppermute(up, "lat", north)
    high_ends = lax.ppermute(down, "lat", south)
    weights = lax.all_gather(weights, "dp", axis=3, tiled=True)
    return (low, high, from_west, from_east, low_ends, high_ends), weights


def body(fields, down_weight, mid_weight, up_weight, cotangent):
    lats, lons, parts = (lax.axis_size(axis) for axis in ("lat", "lon", "dp"))
    _, rows, cols, _ = fields.shape
    half_rows, half_cols = rows // 2, cols // 2
    scale = 1.0 / math.sqrt(parts * rows * lats * cols * lons)
    fields, cotangent = fields[0], cotangent[0]
    weights = jnp.stack([down_weight, mid_weight, up_weight])
    edges, weights = halos(fields, cotangent, weights)
    weights = weights.reshape(3, 9 * C, C)

    slots = half_cols + EDGE
    quads = half_rows // 2 + 5
    pairs = half_rows // 2 + 3
    hbm = pl.BlockSpec(memory_space=pl.ANY)
    inputs = (fields, cotangent, *edges, weights)
    own, other, mid_pairs, grad_pairs = pl.pallas_call(
        functools.partial(grads_kernel, half_rows, half_cols, lats, scale),
        out_shape=(
            jax.ShapeDtypeStruct((TAPS, C // 2, C), F32),
            jax.ShapeDtypeStruct((TAPS, C // 2, C), BF16),
            jax.ShapeDtypeStruct((pairs, 2, half_cols, 2 * C), BF16),
            jax.ShapeDtypeStruct((pairs, 2, half_cols, 2 * C), BF16),
        ),
        in_specs=[hbm] * len(inputs),
        out_specs=(pl.BlockSpec(memory_space=pltpu.VMEM),) * 2
        + (pl.BlockSpec(memory_space=pltpu.HBM),) * 2,
        scratch_shapes=[pltpu.VMEM(array.shape, BF16) for array in inputs]
        + [
            pltpu.VMEM((15 * C, 2 * C), BF16),
            pltpu.VMEM((12 * C, 2 * C), BF16),
            pltpu.VMEM((15 * C, 2 * C), BF16),
            pltpu.VMEM((12 * C, 2 * C), BF16),
            pltpu.VMEM((pairs, 2, half_cols, 2 * C), BF16),
            pltpu.VMEM((pairs, 2, half_cols, 2 * C), BF16),
            pltpu.VMEM((quads, 4, slots, 3 * C), BF16),
            pltpu.VMEM((quads, 4, slots, 3 * C), BF16),
            pltpu.VMEM((pairs + 1, 2, slots, 3 * C), BF16),
            pltpu.VMEM((pairs + 1, 2, slots, 3 * C), BF16),
            pltpu.VMEM((4, cols + 48, C), F32),
            pltpu.VMEM((PAIRS, slots + 16, C), F32),
            pltpu.VMEM((3, C, 9 * C), F32),
            pltpu.SemaphoreType.DMA((6,)),
            pltpu.SemaphoreType.DMA((2, CHUNKS)),
            pltpu.SemaphoreType.DMA,
            pltpu.SemaphoreType.DMA((2,)),
        ],
        compiler_params=pltpu.CompilerParams(vmem_limit_bytes=50 * 2**20),
        cost_estimate=pl.CostEstimate(
            flops=70 * 2 * half_rows * half_cols * C * C,
            transcendentals=half_rows * half_cols * C,
            bytes_accessed=8 * 2**20,
        ),
        name="grads",
    )(*inputs)
    mid_pairs = mid_pairs.reshape(2 * pairs, half_cols, 2 * C)
    grad_pairs = grad_pairs.reshape(2 * pairs, half_cols, 2 * C)

    came = lax.ppermute(other, "dp", [(0, 1), (1, 0)])
    both = (own + came.astype(F32)).astype(BF16)
    pieces = both.reshape(lats * lons, -1, C)
    pieces = lax.all_to_all(pieces, ("lat", "lon"), 0, 0, tiled=True)
    level_out = spread("level", 1, 2, False, mid_pairs, fields, weights)
    piece = jnp.sum(pieces.astype(F32), axis=0, keepdims=True).astype(BF16)
    piece, level_out = lax.optimization_barrier((piece, level_out))
    totals = lax.all_to_all(
        jnp.broadcast_to(piece, pieces.shape), ("lat", "lon"), 0, 0, tiled=True
    )
    _, grad_pairs = lax.optimization_barrier((piece, grad_pairs))
    grad_fields = spread("gradient", 0, 0, True, grad_pairs, cotangent, weights)
    totals = totals.reshape(TAPS, C // 2, C).astype(F32)
    grad_down, grad_mid, grad_up = (
        totals[9 * k : 9 * k + 9].reshape(3, 3, C // 2, C) for k in range(3)
    )
    return (level_out[None], grad_fields[None], grad_down, grad_mid, grad_up)


def solution(mesh):
    field = P("dp", "lat", "lon", None)
    weight = P(None, None, "dp", None)
    return jax.shard_map(
        body,
        mesh=mesh,
        in_specs=(field, weight, weight, weight, field),
        out_specs=(field, field, weight, weight, weight),
        check_vma=False,
    )
```

```python
import functools
import math

import jax
import jax.numpy as jnp
from jax import lax
from jax.experimental import pallas as pl
from jax.experimental.pallas import tpu as pltpu
from jax.sharding import PartitionSpec as P

BF16 = jnp.bfloat16
F32 = jnp.float32
C = 128
FIELD_LOW, FIELD_HIGH = 5, 6
COT_LOW, COT_HIGH = 3, 4
ROWS = 5
PAIRS = 12
CELL_PAIRS = 10
CHUNKS = 4
EDGE = 16
LOW_ENDS, HIGH_ENDS = 2 * FIELD_LOW + 2, 2 * FIELD_HIGH + 2
TAPS = 32


def dot(left, right):
    return jnp.dot(left, right, preferred_element_type=F32)


def flat(value):
    return value.reshape(-1, value.shape[-1])


def split_row(stage, row, dest, block, place, west, *easts):
    wide = row.shape[0]
    stage[24 - west.shape[0] : 24, :] = west.astype(F32)
    stage[24 : 24 + wide, :] = row.astype(F32)
    at = 24 + wide
    for east in easts:
        stage[at : at + east.shape[0], :] = east.astype(F32)
        at += east.shape[0]
    own = wide // 2 + 8
    for tap in range(3):
        upper = stage[pl.ds(23 + tap, own, stride=2), :]
        lower = stage[pl.ds(7 + tap, 8, stride=2), :]
        dest[block, place, :, tap * C : (tap + 1) * C] = jnp.concatenate(
            [upper, lower], axis=0
        ).astype(BF16)


def joined(refs, count, first, offsets):
    return jnp.concatenate(
        [flat(refs[pl.ds(first + block, count), place]) for block, place in offsets], axis=1
    )


def grads_kernel(
    half_rows,
    half_cols,
    bands,
    scale,
    fields_hbm,
    cot_hbm,
    low_hbm,
    high_hbm,
    west_hbm,
    east_hbm,
    low_ends_hbm,
    high_ends_hbm,
    weights_hbm,
    own_out,
    other_out,
    mid_out,
    grad_out,
    fields,
    cot,
    low,
    high,
    west,
    east,
    low_ends,
    high_ends,
    weights,
    p_down,
    p_mid,
    p_up_t,
    p_mid_t,
    mid_pairs,
    grad_pairs,
    field_taps,
    cot_taps,
    down_taps,
    pre_taps,
    stage,
    line,
    acc,
    edge_sems,
    own_sems,
    weight_sem,
    out_sems,
):
    lat, part = lax.axis_index("lat"), lax.axis_index("dp")
    slots = half_cols + EDGE
    wide = half_cols + 8
    rows = 2 * half_rows
    chunk = rows // CHUNKS

    edge_copies = [
        pltpu.make_async_copy(source, dest, edge_sems.at[k])
        for k, (source, dest) in enumerate(
            [
                (low_hbm, low),
                (high_hbm, high),
                (west_hbm, west),
                (east_hbm, east),
                (low_ends_hbm, low_ends),
                (high_ends_hbm, high_ends),
            ]
        )
    ]
    own_copies = [
        pltpu.make_async_copy(
            source.at[pl.ds(n * chunk, chunk)], dest.at[pl.ds(n * chunk, chunk)], own_sems.at[k, n]
        )
        for n in range(CHUNKS)
        for k, (source, dest) in enumerate([(fields_hbm, fields), (cot_hbm, cot)])
    ]
    weight_copy = pltpu.make_async_copy(weights_hbm, weights, weight_sem)
    for copy in edge_copies + own_copies + [weight_copy]:
        copy.start()
    acc[...] = jnp.zeros_like(acc)
    for packed in (p_down, p_mid, p_up_t, p_mid_t):
        packed[...] = jnp.zeros_like(packed)
    for copy in edge_copies:
        copy.wait()

    def end_rows(rows_in, ends, fields_in, cots_in, row_of_cot, first_row, field_at, cot_at):
        for k in range(fields_in):
            split_row(
                stage.at[k % 4],
                rows_in[k],
                field_taps,
                (field_at + k) // 4,
                (field_at + k) % 4,
                ends[k],
                ends[fields_in + k],
            )
        for k in range(cots_in):
            end = row_of_cot + k
            spare = 2 * ((first_row + end) % 4)
            split_row(
                stage.at[k % 4],
                rows_in[fields_in + k],
                cot_taps,
                (cot_at + k) // 4,
                (cot_at + k) % 4,
                ends[end, :COT_LOW],
                ends[fields_in + end, FIELD_HIGH:],
                ends[2 * fields_in + (first_row % 4 + end) // 4, spare : spare + 2],
            )

    end_rows(low, low_ends, FIELD_LOW, COT_LOW, FIELD_LOW - COT_LOW, rows - FIELD_LOW, 0, 0)
    end_rows(high, high_ends, FIELD_HIGH, COT_HIGH, 0, 0, FIELD_LOW + rows, COT_LOW + rows)

    def own_rows(t, carry):
        for k in range(4):
            q, p = 4 * t + k, FIELD_LOW + k
            split_row(stage.at[k], fields[q], field_taps, t + p // 4, p % 4, west[q], east[q])
        for k in range(4):
            q, p = 4 * t + k, COT_LOW + k
            split_row(
                stage.at[k],
                cot[q],
                cot_taps,
                t + p // 4,
                p % 4,
                west[q, :COT_LOW],
                east[q, FIELD_HIGH:],
                east[rows + t, 2 * k : 2 * k + 2],
            )
        return carry

    for n in range(CHUNKS):
        own_copies[2 * n].wait()
        own_copies[2 * n + 1].wait()
        lax.fori_loop(n * chunk // 4, (n + 1) * chunk // 4, own_rows, 0)

    weight_copy.wait()
    for kind, packed, apart, swapped, turned in (
        (0, p_down, 2, False, False),
        (1, p_mid, 1, False, False),
        (2, p_up_t, 2, True, False),
        (1, p_mid_t, 1, True, True),
    ):
        for tap in range(9):
            held = (8 - tap if turned else tap) * C
            block = weights[kind, held : held + C, :]
            block = block.T if swapped else block
            for odd in range(2):
                at = (odd * apart * 3 + tap) * C
                packed[at : at + C, odd * C : (odd + 1) * C] = block

    def on_grid(value, first):
        at = lat * half_rows + first + 2 * lax.broadcasted_iota(jnp.int32, value.shape, 0)
        return jnp.where((at >= 0) & (at < bands * half_rows), value, 0.0)

    def lay(value):
        count = value.shape[0]
        line[:count, 8:16, :] = value[:, wide:]
        line[:count, 16 : 16 + wide, :] = value[:, :wide]

    def shifted(count, shift):
        upper = line[:count, 16 + shift : 16 + shift + wide, :]
        lower = line[:count, 8 + shift : 16 + shift, :]
        return jnp.concatenate([upper, lower], axis=1).astype(BF16)

    def keep_three(dest, at, odd, count, value):
        lay(value)
        for shift in range(3):
            dest[pl.ds(at, count), odd, :, shift * C : (shift + 1) * C] = shifted(count, shift - 1)

    def keep_two(dest, at, odd, count, value):
        lay(value)
        for shift in range(2):
            dest[pl.ds(at, count), odd, :, shift * C : (shift + 1) * C] = line[
                :count, 16 + shift : 16 + shift + half_cols, :
            ].astype(BF16)

    def both_rows(value, count):
        return [value[:, odd * C : (odd + 1) * C].reshape(count, slots, C) for odd in range(2)]

    near = [(q // 2, q % 2) for q in range(4)]
    fine = [(q // 4, q % 4) for q in range(5)]

    def over_pairs(total, work):
        lax.fori_loop(0, total // PAIRS, lambda t, carry: (work(PAIRS * t, PAIRS), carry)[1], 0)
        if total % PAIRS:
            work(total // PAIRS * PAIRS, total % PAIRS)

    def down_strip(m, count):
        values = both_rows(dot(joined(field_taps, count, m, fine), p_down[...]), count)
        for odd, value in enumerate(values):
            keep_three(down_taps, m, odd, count, on_grid(value, 2 * m + odd - 2))

    def pre_strip(m, count):
        pres = both_rows(dot(joined(down_taps, count, m, near), p_mid[...]), count)
        grads = both_rows(dot(joined(cot_taps, count, m, fine), p_up_t[...]), count)
        for odd in range(2):
            pre, grad, first = pres[odd], grads[odd], 2 * m + odd - 1
            sig = jax.nn.sigmoid(pre)
            keep_two(mid_pairs, m, odd, count, on_grid(pre * sig, first))
            keep_three(
                pre_taps, m, odd, count, on_grid(grad * sig * (1.0 + pre * (1.0 - sig)), first)
            )

    def back_strip(m, count):
        values = both_rows(dot(joined(pre_taps, count, m, near), p_mid_t[...]), count)
        for odd, value in enumerate(values):
            keep_two(grad_pairs, m, odd, count, on_grid(value, 2 * m + odd))

    over_pairs(half_rows // 2 + 3, down_strip)
    over_pairs(half_rows // 2 + 2, pre_strip)
    mid_copy = pltpu.make_async_copy(mid_pairs, mid_out, out_sems.at[0])
    mid_copy.start()
    over_pairs(half_rows // 2 + 1, back_strip)
    grad_copy = pltpu.make_async_copy(grad_pairs, grad_out, out_sems.at[1])
    grad_copy.start()

    here = slice(0, half_cols)

    def outer(kind, left, right):
        left = jnp.concatenate([flat(piece) for piece in left], axis=0)
        right = jnp.concatenate(
            [jnp.concatenate([flat(piece) for piece in pieces], axis=1) for pieces in right], axis=0
        )
        acc[kind] += lax.dot_general(
            left, right, (((0,), (0,)), ((), ())), preferred_element_type=F32
        )

    def outer_strip(t, carry):
        m = CELL_PAIRS * t

        def piece(ref, cells, every, row):
            return ref[pl.ds(m + row // every, CELL_PAIRS), row % every, here, cells]

        every_lane, middle, first_lane = slice(None), slice(C, 2 * C), slice(0, C)
        outer(
            0,
            [piece(grad_pairs, first_lane, 2, odd) for odd in range(2)],
            [[piece(field_taps, every_lane, 4, 4 + 2 * odd + r) for r in range(3)] for odd in range(2)],
        )
        outer(
            1,
            [piece(down_taps, middle, 2, 2 + odd) for odd in range(2)],
            [[piece(pre_taps, every_lane, 2, odd + r) for r in range(3)] for odd in range(2)],
        )
        outer(
            2,
            [piece(mid_pairs, first_lane, 2, 1 + odd) for odd in range(2)],
            [[piece(cot_taps, every_lane, 4, 2 + 2 * odd + r) for r in range(3)] for odd in range(2)],
        )
        return carry

    lax.fori_loop(0, half_rows // (2 * CELL_PAIRS), outer_strip, 0)

    half = C // 2
    for tap in range(9):
        at = slice(tap * C, (tap + 1) * C)
        acc[0, :, at] = acc[0, :, at].T
    mine = pl.ds(pl.multiple_of(part * half, half), half)
    theirs = pl.ds(pl.multiple_of((1 - part) * half, half), half)
    for kind in range(3):
        for tap in range(9):
            held = 8 - tap if kind == 1 else tap
            at = slice(held * C, (held + 1) * C)
            own_out[kind * 9 + tap] = acc[kind, mine, at] * scale
            other_out[kind * 9 + tap] = (acc[kind, theirs, at] * scale).astype(BF16)
    for tap in range(27, TAPS):
        own_out[tap] = jnp.zeros((half, C), F32)
        other_out[tap] = jnp.zeros((half, C), BF16)
    mid_copy.wait()
    grad_copy.wait()


def up_kernel(
    above,
    kind,
    swapped,
    pairs_hbm,
    base_hbm,
    weights_hbm,
    out_hbm,
    pairs,
    base,
    kernel,
    out,
    whole,
    in_sems,
    out_sems,
):
    half_cols = pairs.shape[1]
    fine = 2 * ROWS
    strips = base.shape[0] // fine
    whole_copies = [
        pltpu.make_async_copy(source, dest, in_sems.at[strips + k])
        for k, (source, dest) in enumerate([(weights_hbm.at[kind], kernel), (pairs_hbm, pairs)])
    ]

    def rows(n):
        return pl.ds(n * fine, fine)

    base_copies = [
        pltpu.make_async_copy(base_hbm.at[rows(n)], base.at[rows(n)], in_sems.at[n])
        for n in range(strips)
    ]
    out_copies = [
        pltpu.make_async_copy(out.at[rows(n)], out_hbm.at[rows(n)], out_sems.at[n])
        for n in range(strips)
    ]
    for copy in whole_copies + base_copies:
        copy.start()
    for copy in whole_copies:
        copy.wait()

    def tap(row, col):
        k = 3 * row + col
        block = kernel[k * C : (k + 1) * C, :]
        return block.T if swapped else block

    def lanes(*pieces):
        return jnp.concatenate(pieces, axis=1)

    odd_kernel = jnp.concatenate([lanes(tap(1, 2), tap(2, 2)), lanes(tap(1, 0), tap(2, 0))], axis=0)
    last_kernel = jnp.concatenate([tap(0, 2), tap(0, 0)], axis=0)
    even_kernel = jnp.concatenate(
        [lanes(tap(1, 1), tap(2, 1)), lanes(jnp.zeros((C, C), BF16), tap(0, 1))], axis=0
    )
    for n in range(strips):
        at = ROWS * n + above
        near = flat(pairs[at : at + ROWS])
        far = flat(pairs[at + 1 : at + 1 + ROWS])
        odd = dot(near, odd_kernel)
        last = dot(far, last_kernel)
        even = dot(lanes(near[:, :C], far[:, :C]), even_kernel)
        for k in range(ROWS):
            at_k = slice(k * half_cols, (k + 1) * half_cols)
            whole[2 * k, pl.ds(0, half_cols, stride=2), :] = even[at_k, :C]
            whole[2 * k, pl.ds(1, half_cols, stride=2), :] = odd[at_k, :C]
            whole[2 * k + 1, pl.ds(0, half_cols, stride=2), :] = even[at_k, C:]
            whole[2 * k + 1, pl.ds(1, half_cols, stride=2), :] = odd[at_k, C:] + last[at_k]
        base_copies[n].wait()
        out[rows(n)] = (base[rows(n)].astype(F32) + whole[...]).astype(BF16)
        out_copies[n].start()
    for copy in out_copies:
        copy.wait()


def spread(name, above, kind, swapped, pairs, base, weights):
    rows, cols, _ = base.shape
    strips = rows // (2 * ROWS)
    hbm = pl.BlockSpec(memory_space=pltpu.HBM)
    return pl.pallas_call(
        functools.partial(up_kernel, above, kind, swapped),
        out_shape=jax.ShapeDtypeStruct(base.shape, BF16),
        in_specs=[hbm] * 3,
        out_specs=hbm,
        scratch_shapes=[
            pltpu.VMEM(shape, BF16)
            for shape in (pairs.shape, base.shape, weights.shape[1:], base.shape)
        ]
        + [
            pltpu.VMEM((2 * ROWS, cols, C), F32),
            pltpu.SemaphoreType.DMA((strips + 2,)),
            pltpu.SemaphoreType.DMA((strips,)),
        ],
        compiler_params=pltpu.CompilerParams(vmem_limit_bytes=60 * 2**20),
        cost_estimate=pl.CostEstimate(
            flops=9 * rows * cols * C * C // 2, transcendentals=0, bytes_accessed=7 * 2**20
        ),
        name=name,
    )(pairs, base, weights)


def copied(name, out_shapes, moves, limit, *arrays):
    def kernel(*refs):
        ins, outs, sems = refs[: len(arrays)], refs[len(arrays) : -1], refs[-1]
        copies = [
            pltpu.make_async_copy(ins[i].at[cut], outs[o].at[place], sems.at[k])
            for k, (i, cut, o, place) in enumerate(moves)
        ]
        for copy in copies:
            copy.start()
        for copy in copies:
            copy.wait()

    return pl.pallas_call(
        kernel,
        out_shape=tuple(jax.ShapeDtypeStruct(shape, BF16) for shape in out_shapes),
        in_specs=[pl.BlockSpec(memory_space=pl.ANY)] * len(arrays),
        out_specs=(pl.BlockSpec(memory_space=pltpu.VMEM),) * len(out_shapes),
        scratch_shapes=[pltpu.SemaphoreType.DMA((len(moves),))],
        compiler_params=pltpu.CompilerParams(vmem_limit_bytes=limit * 2**20),
        name=name,
    )(*arrays)


def pack_kernel(fields_hbm, cot_hbm, east, west, up, down, ends, spare, sems):
    rows, cols, _ = fields_hbm.shape
    column_copies = [
        pltpu.make_async_copy(source.at[:, pl.ds(at, 8), :], ends.at[k], sems.at[k])
        for k, (source, at) in enumerate(
            [(fields_hbm, cols - 8), (cot_hbm, cols - 8), (fields_hbm, 0), (cot_hbm, 0)]
        )
    ]
    row_copies = [
        pltpu.make_async_copy(
            source.at[pl.ds(at, count)], dest.at[pl.ds(place, count)], sems.at[4 + k]
        )
        for k, (source, at, count, dest, place) in enumerate(
            [
                (fields_hbm, rows - FIELD_LOW, FIELD_LOW, up, 0),
                (cot_hbm, rows - COT_LOW, COT_LOW, up, FIELD_LOW),
                (fields_hbm, 0, FIELD_HIGH, down, 0),
                (cot_hbm, 0, COT_HIGH, down, FIELD_HIGH),
            ]
        )
    ]
    for copy in column_copies + row_copies:
        copy.start()
    for copy in column_copies:
        copy.wait()
    field, other = ends[0].astype(F32), ends[1].astype(F32)
    east[...] = jnp.concatenate(
        [other[:, 8 - COT_LOW :], field[:, 8 - FIELD_LOW :]], axis=1
    ).astype(BF16)
    field, other = ends[2].astype(F32), ends[3].astype(F32)
    beside = 8 - FIELD_HIGH
    west[:rows] = jnp.concatenate([field[:, :FIELD_HIGH], other[:, :beside]], axis=1).astype(BF16)
    other = other.reshape(rows // 4, 4, 8, C)
    for k in range(4):
        spare[:, 2 * k : 2 * k + 2, :] = other[:, k, beside:COT_HIGH]
    west[rows:] = spare[...].astype(BF16)
    for copy in row_copies:
        copy.wait()


def packed(fields, cot):
    rows, cols, _ = fields.shape
    vmem = pl.BlockSpec(memory_space=pltpu.VMEM)
    return pl.pallas_call(
        pack_kernel,
        out_shape=(
            jax.ShapeDtypeStruct((rows, 8, C), BF16),
            jax.ShapeDtypeStruct((rows + rows // 4, 8, C), BF16),
            jax.ShapeDtypeStruct((FIELD_LOW + COT_LOW, cols, C), BF16),
            jax.ShapeDtypeStruct((FIELD_HIGH + COT_HIGH, cols, C), BF16),
        ),
        in_specs=[pl.BlockSpec(memory_space=pl.ANY)] * 2,
        out_specs=(vmem,) * 4,
        scratch_shapes=[
            pltpu.VMEM((4, rows, 8, C), BF16),
            pltpu.VMEM((rows // 4, 8, C), F32),
            pltpu.SemaphoreType.DMA((8,)),
        ],
        compiler_params=pltpu.CompilerParams(vmem_limit_bytes=52 * 2**20),
        name="pack",
    )(fields, cot)


def passed(*arrays):
    hbm = pl.BlockSpec(memory_space=pl.ANY)
    return pl.pallas_call(
        lambda *refs: None,
        out_shape=tuple(jax.ShapeDtypeStruct(array.shape, array.dtype) for array in arrays),
        in_specs=[hbm] * len(arrays),
        out_specs=(hbm,) * len(arrays),
        input_output_aliases={k: k for k in range(len(arrays))},
        compiler_params=pltpu.CompilerParams(vmem_limit_bytes=2**20),
        name="passed",
    )(*arrays)


def halos(fields, cot, weights):
    lat = lax.axis_size("lat")
    lon = lax.axis_size("lon")
    rows = fields.shape[0]
    every = slice(None)

    def row(start, count):
        return (pl.ds(start, count), every, every)

    east, west, up, down = packed(fields, cot)
    up, down = passed(up, down)
    north = [(i, i + 1) for i in range(lat - 1)]
    south = [(j, i) for i, j in north]
    eastward = [(i, (i + 1) % lon) for i in range(lon)]
    westward = [(j, i) for i, j in eastward]
    from_west = lax.ppermute(east, "lon", eastward)
    from_east = lax.ppermute(west, "lon", westward)
    low = lax.ppermute(up, "lat", north)
    high = lax.ppermute(down, "lat", south)
    spare = rows + (rows - FIELD_LOW) // 4
    up, down = copied(
        "corners",
        [(LOW_ENDS, 8, C), (HIGH_ENDS, 8, C)],
        [
            (0, row(rows - FIELD_LOW, FIELD_LOW), 0, row(0, FIELD_LOW)),
            (1, row(rows - FIELD_LOW, FIELD_LOW), 0, row(FIELD_LOW, FIELD_LOW)),
            (1, row(spare, 2), 0, row(2 * FIELD_LOW, 2)),
            (0, row(0, FIELD_HIGH), 1, row(0, FIELD_HIGH)),
            (1, row(0, FIELD_HIGH), 1, row(FIELD_HIGH, FIELD_HIGH)),
            (1, row(rows, 2), 1, row(2 * FIELD_HIGH, 2)),
        ],
        2,
        from_west,
        from_east,
    )
    up, down, weights = lax.optimization_barrier((up, down, weights))
    low_ends = lax.ppermute(up, "lat", north)
    high_ends = lax.ppermute(down, "lat", south)
    weights = lax.all_gather(weights, "dp", axis=3, tiled=True)
    return (low, high, from_west, from_east, low_ends, high_ends), weights


def body(fields, down_weight, mid_weight, up_weight, cotangent):
    lats, lons, parts = (lax.axis_size(axis) for axis in ("lat", "lon", "dp"))
    _, rows, cols, _ = fields.shape
    half_rows, half_cols = rows // 2, cols // 2
    scale = 1.0 / math.sqrt(parts * rows * lats * cols * lons)
    fields, cotangent = fields[0], cotangent[0]
    weights = jnp.stack([down_weight, mid_weight, up_weight])
    edges, weights = halos(fields, cotangent, weights)
    weights = weights.reshape(3, 9 * C, C)

    slots = half_cols + EDGE
    quads = half_rows // 2 + 5
    pairs = half_rows // 2 + 3
    hbm = pl.BlockSpec(memory_space=pl.ANY)
    inputs = (fields, cotangent, *edges, weights)
    own, other, mid_pairs, grad_pairs = pl.pallas_call(
        functools.partial(grads_kernel, half_rows, half_cols, lats, scale),
        out_shape=(
            jax.ShapeDtypeStruct((TAPS, C // 2, C), F32),
            jax.ShapeDtypeStruct((TAPS, C // 2, C), BF16),
            jax.ShapeDtypeStruct((pairs, 2, half_cols, 2 * C), BF16),
            jax.ShapeDtypeStruct((pairs, 2, half_cols, 2 * C), BF16),
        ),
        in_specs=[hbm] * len(inputs),
        out_specs=(pl.BlockSpec(memory_space=pltpu.VMEM),) * 2
        + (pl.BlockSpec(memory_space=pltpu.HBM),) * 2,
        scratch_shapes=[pltpu.VMEM(array.shape, BF16) for array in inputs]
        + [
            pltpu.VMEM((15 * C, 2 * C), BF16),
            pltpu.VMEM((12 * C, 2 * C), BF16),
            pltpu.VMEM((15 * C, 2 * C), BF16),
            pltpu.VMEM((12 * C, 2 * C), BF16),
            pltpu.VMEM((pairs, 2, half_cols, 2 * C), BF16),
            pltpu.VMEM((pairs, 2, half_cols, 2 * C), BF16),
            pltpu.VMEM((quads, 4, slots, 3 * C), BF16),
            pltpu.VMEM((quads, 4, slots, 3 * C), BF16),
            pltpu.VMEM((pairs + 1, 2, slots, 3 * C), BF16),
            pltpu.VMEM((pairs + 1, 2, slots, 3 * C), BF16),
            pltpu.VMEM((4, cols + 48, C), F32),
            pltpu.VMEM((PAIRS, slots + 16, C), F32),
            pltpu.VMEM((3, C, 9 * C), F32),
            pltpu.SemaphoreType.DMA((6,)),
            pltpu.SemaphoreType.DMA((2, CHUNKS)),
            pltpu.SemaphoreType.DMA,
            pltpu.SemaphoreType.DMA((2,)),
        ],
        compiler_params=pltpu.CompilerParams(vmem_limit_bytes=50 * 2**20),
        cost_estimate=pl.CostEstimate(
            flops=70 * 2 * half_rows * half_cols * C * C,
            transcendentals=half_rows * half_cols * C,
            bytes_accessed=8 * 2**20,
        ),
        name="grads",
    )(*inputs)
    mid_pairs = mid_pairs.reshape(2 * pairs, half_cols, 2 * C)
    grad_pairs = grad_pairs.reshape(2 * pairs, half_cols, 2 * C)

    came = lax.ppermute(other, "dp", [(0, 1), (1, 0)])
    both = (own + came.astype(F32)).astype(BF16)
    pieces = both.reshape(lats * lons, -1, C)
    pieces = lax.all_to_all(pieces, ("lat", "lon"), 0, 0, tiled=True)
    piece = jnp.sum(pieces.astype(F32), axis=0, keepdims=True).astype(BF16)
    totals = lax.all_to_all(
        jnp.broadcast_to(piece, pieces.shape), ("lat", "lon"), 0, 0, tiled=True
    )
    _, mid_pairs, grad_pairs = lax.optimization_barrier((piece, mid_pairs, grad_pairs))
    level_out = spread("level", 1, 2, False, mid_pairs, fields, weights)
    grad_fields = spread("gradient", 0, 0, True, grad_pairs, cotangent, weights)
    totals = totals.reshape(TAPS, C // 2, C).astype(F32)
    grad_down, grad_mid, grad_up = (
        totals[9 * k : 9 * k + 9].reshape(3, 3, C // 2, C) for k in range(3)
    )
    return (level_out[None], grad_fields[None], grad_down, grad_mid, grad_up)


def solution(mesh):
    field = P("dp", "lat", "lon", None)
    weight = P(None, None, "dp", None)
    return jax.shard_map(
        body,
        mesh=mesh,
        in_specs=(field, weight, weight, weight, field),
        out_specs=(field, field, weight, weight, weight),
        check_vma=False,
    )
```

```python
import functools
import math

import jax
import jax.numpy as jnp
from jax import lax
from jax.experimental import pallas as pl
from jax.experimental.pallas import tpu as pltpu
from jax.sharding import PartitionSpec as P

BF16 = jnp.bfloat16
F32 = jnp.float32
C = 128
FIELD_LOW, FIELD_HIGH = 5, 6
COT_LOW, COT_HIGH = 3, 4
ROWS = 5
PAIRS = 12
CELL_PAIRS = 10
CHUNKS = 4
EDGE = 16
LOW_ENDS, HIGH_ENDS = 2 * FIELD_LOW + 2, 2 * FIELD_HIGH + 2
TAPS = 32


def dot(left, right):
    return jnp.dot(left, right, preferred_element_type=F32)


def flat(value):
    return value.reshape(-1, value.shape[-1])


def split_row(stage, row, dest, block, place, west, *easts):
    wide = row.shape[0]
    stage[24 - west.shape[0] : 24, :] = west.astype(F32)
    stage[24 : 24 + wide, :] = row.astype(F32)
    at = 24 + wide
    for east in easts:
        stage[at : at + east.shape[0], :] = east.astype(F32)
        at += east.shape[0]
    own = wide // 2 + 8
    for tap in range(3):
        upper = stage[pl.ds(23 + tap, own, stride=2), :]
        lower = stage[pl.ds(7 + tap, 8, stride=2), :]
        dest[block, place, :, tap * C : (tap + 1) * C] = jnp.concatenate(
            [upper, lower], axis=0
        ).astype(BF16)


def joined(refs, count, first, offsets):
    return jnp.concatenate(
        [flat(refs[pl.ds(first + block, count), place]) for block, place in offsets], axis=1
    )


def grads_kernel(
    half_rows,
    half_cols,
    bands,
    scale,
    fields_hbm,
    cot_hbm,
    low_hbm,
    high_hbm,
    west_hbm,
    east_hbm,
    low_ends_hbm,
    high_ends_hbm,
    weights_hbm,
    own_out,
    other_out,
    mid_out,
    grad_out,
    fields,
    cot,
    low,
    high,
    west,
    east,
    low_ends,
    high_ends,
    weights,
    p_down,
    p_mid,
    p_up_t,
    p_mid_t,
    mid_pairs,
    grad_pairs,
    field_taps,
    cot_taps,
    down_taps,
    pre_taps,
    stage,
    line,
    acc,
    edge_sems,
    own_sems,
    weight_sem,
    out_sems,
):
    lat, part = lax.axis_index("lat"), lax.axis_index("dp")
    slots = half_cols + EDGE
    wide = half_cols + 8
    rows = 2 * half_rows
    chunk = rows // CHUNKS

    edge_copies = [
        pltpu.make_async_copy(source, dest, edge_sems.at[k])
        for k, (source, dest) in enumerate(
            [
                (low_hbm, low),
                (high_hbm, high),
                (west_hbm, west),
                (east_hbm, east),
                (low_ends_hbm, low_ends),
                (high_ends_hbm, high_ends),
            ]
        )
    ]
    own_copies = [
        pltpu.make_async_copy(
            source.at[pl.ds(n * chunk, chunk)], dest.at[pl.ds(n * chunk, chunk)], own_sems.at[k, n]
        )
        for n in range(CHUNKS)
        for k, (source, dest) in enumerate([(fields_hbm, fields), (cot_hbm, cot)])
    ]
    weight_copy = pltpu.make_async_copy(weights_hbm, weights, weight_sem)
    for copy in edge_copies + own_copies + [weight_copy]:
        copy.start()
    acc[...] = jnp.zeros_like(acc)
    for packed in (p_down, p_mid, p_up_t, p_mid_t):
        packed[...] = jnp.zeros_like(packed)
    for taps, end in (
        (field_taps, FIELD_LOW + rows + FIELD_HIGH),
        (cot_taps, COT_LOW + rows + COT_HIGH),
    ):
        for p in (end, end + 1):
            taps[p // 4, p % 4] = jnp.zeros((slots, 3 * C), BF16)
    for copy in edge_copies:
        copy.wait()

    def end_rows(rows_in, ends, fields_in, cots_in, row_of_cot, first_row, field_at, cot_at):
        for k in range(fields_in):
            split_row(
                stage.at[k % 4],
                rows_in[k],
                field_taps,
                (field_at + k) // 4,
                (field_at + k) % 4,
                ends[k],
                ends[fields_in + k],
            )
        for k in range(cots_in):
            end = row_of_cot + k
            spare = 2 * ((first_row + end) % 4)
            split_row(
                stage.at[k % 4],
                rows_in[fields_in + k],
                cot_taps,
                (cot_at + k) // 4,
                (cot_at + k) % 4,
                ends[end, :COT_LOW],
                ends[fields_in + end, FIELD_HIGH:],
                ends[2 * fields_in + (first_row % 4 + end) // 4, spare : spare + 2],
            )

    end_rows(low, low_ends, FIELD_LOW, COT_LOW, FIELD_LOW - COT_LOW, rows - FIELD_LOW, 0, 0)
    end_rows(high, high_ends, FIELD_HIGH, COT_HIGH, 0, 0, FIELD_LOW + rows, COT_LOW + rows)

    def own_rows(t, carry):
        for k in range(4):
            q, p = 4 * t + k, FIELD_LOW + k
            split_row(stage.at[k], fields[q], field_taps, t + p // 4, p % 4, west[q], east[q])
        for k in range(4):
            q, p = 4 * t + k, COT_LOW + k
            split_row(
                stage.at[k],
                cot[q],
                cot_taps,
                t + p // 4,
                p % 4,
                west[q, :COT_LOW],
                east[q, FIELD_HIGH:],
                east[rows + t, 2 * k : 2 * k + 2],
            )
        return carry

    for n in range(CHUNKS):
        own_copies[2 * n].wait()
        own_copies[2 * n + 1].wait()
        lax.fori_loop(n * chunk // 4, (n + 1) * chunk // 4, own_rows, 0)

    weight_copy.wait()
    for kind, packed, apart, swapped, turned in (
        (0, p_down, 2, False, False),
        (1, p_mid, 1, False, False),
        (2, p_up_t, 2, True, False),
        (1, p_mid_t, 1, True, True),
    ):
        for tap in range(9):
            held = (8 - tap if turned else tap) * C
            block = weights[kind, held : held + C, :]
            block = block.T if swapped else block
            for odd in range(2):
                at = (odd * apart * 3 + tap) * C
                packed[at : at + C, odd * C : (odd + 1) * C] = block

    def on_grid(value, first):
        at = lat * half_rows + first + 2 * lax.broadcasted_iota(jnp.int32, value.shape, 0)
        return jnp.where((at >= 0) & (at < bands * half_rows), value, 0.0)

    def lay(value):
        count = value.shape[0]
        line[:count, 8:16, :] = value[:, wide:]
        line[:count, 16 : 16 + wide, :] = value[:, :wide]

    def shifted(count, shift):
        upper = line[:count, 16 + shift : 16 + shift + wide, :]
        lower = line[:count, 8 + shift : 16 + shift, :]
        return jnp.concatenate([upper, lower], axis=1).astype(BF16)

    def keep_three(dest, at, odd, count, value):
        lay(value)
        for shift in range(3):
            dest[pl.ds(at, count), odd, :, shift * C : (shift + 1) * C] = shifted(count, shift - 1)

    def keep_two(dest, at, odd, count, value):
        lay(value)
        for shift in range(2):
            dest[pl.ds(at, count), odd, :, shift * C : (shift + 1) * C] = line[
                :count, 16 + shift : 16 + shift + half_cols, :
            ].astype(BF16)

    def both_rows(value, count):
        return [value[:, odd * C : (odd + 1) * C].reshape(count, slots, C) for odd in range(2)]

    near = [(q // 2, q % 2) for q in range(4)]
    fine = [(q // 4, q % 4) for q in range(5)]

    def over_pairs(total, work):
        lax.fori_loop(0, total // PAIRS, lambda t, carry: (work(PAIRS * t, PAIRS), carry)[1], 0)
        if total % PAIRS:
            work(total // PAIRS * PAIRS, total % PAIRS)

    def down_strip(m, count):
        values = both_rows(dot(joined(field_taps, count, m, fine), p_down[...]), count)
        for odd, value in enumerate(values):
            keep_three(down_taps, m, odd, count, on_grid(value, 2 * m + odd - 2))

    def pre_strip(m, count):
        pres = both_rows(dot(joined(down_taps, count, m, near), p_mid[...]), count)
        grads = both_rows(dot(joined(cot_taps, count, m, fine), p_up_t[...]), count)
        for odd in range(2):
            pre, grad, first = pres[odd], grads[odd], 2 * m + odd - 1
            sig = jax.nn.sigmoid(pre)
            keep_two(mid_pairs, m, odd, count, on_grid(pre * sig, first))
            keep_three(
                pre_taps, m, odd, count, on_grid(grad * sig * (1.0 + pre * (1.0 - sig)), first)
            )

    def back_strip(m, count):
        values = both_rows(dot(joined(pre_taps, count, m, near), p_mid_t[...]), count)
        for odd, value in enumerate(values):
            keep_two(grad_pairs, m, odd, count, on_grid(value, 2 * m + odd))

    over_pairs(half_rows // 2 + 3, down_strip)
    over_pairs(half_rows // 2 + 2, pre_strip)
    mid_copy = pltpu.make_async_copy(mid_pairs, mid_out, out_sems.at[0])
    mid_copy.start()
    over_pairs(half_rows // 2 + 1, back_strip)
    grad_copy = pltpu.make_async_copy(grad_pairs, grad_out, out_sems.at[1])
    grad_copy.start()

    here = slice(0, half_cols)

    def outer(kind, left, right):
        left = jnp.concatenate([flat(piece) for piece in left], axis=0)
        right = jnp.concatenate(
            [jnp.concatenate([flat(piece) for piece in pieces], axis=1) for pieces in right], axis=0
        )
        acc[kind] += lax.dot_general(
            left, right, (((0,), (0,)), ((), ())), preferred_element_type=F32
        )

    def outer_strip(t, carry):
        m = CELL_PAIRS * t

        def piece(ref, cells, every, row):
            return ref[pl.ds(m + row // every, CELL_PAIRS), row % every, here, cells]

        every_lane, middle, first_lane = slice(None), slice(C, 2 * C), slice(0, C)
        outer(
            0,
            [piece(grad_pairs, first_lane, 2, odd) for odd in range(2)],
            [[piece(field_taps, every_lane, 4, 4 + 2 * odd + r) for r in range(3)] for odd in range(2)],
        )
        outer(
            1,
            [piece(down_taps, middle, 2, 2 + odd) for odd in range(2)],
            [[piece(pre_taps, every_lane, 2, odd + r) for r in range(3)] for odd in range(2)],
        )
        outer(
            2,
            [piece(mid_pairs, first_lane, 2, 1 + odd) for odd in range(2)],
            [[piece(cot_taps, every_lane, 4, 2 + 2 * odd + r) for r in range(3)] for odd in range(2)],
        )
        return carry

    lax.fori_loop(0, half_rows // (2 * CELL_PAIRS), outer_strip, 0)

    half = C // 2
    for tap in range(9):
        at = slice(tap * C, (tap + 1) * C)
        acc[0, :, at] = acc[0, :, at].T
    mine = pl.ds(pl.multiple_of(part * half, half), half)
    theirs = pl.ds(pl.multiple_of((1 - part) * half, half), half)
    for kind in range(3):
        for tap in range(9):
            held = 8 - tap if kind == 1 else tap
            at = slice(held * C, (held + 1) * C)
            own_out[kind * 9 + tap] = acc[kind, mine, at] * scale
            other_out[kind * 9 + tap] = (acc[kind, theirs, at] * scale).astype(BF16)
    for tap in range(27, TAPS):
        own_out[tap] = jnp.zeros((half, C), F32)
        other_out[tap] = jnp.zeros((half, C), BF16)
    mid_copy.wait()
    grad_copy.wait()


def up_kernel(
    above,
    kind,
    swapped,
    pairs_hbm,
    base_hbm,
    weights_hbm,
    out_hbm,
    pairs,
    base,
    kernel,
    out,
    whole,
    in_sems,
    out_sems,
):
    half_cols = pairs.shape[1]
    fine = 2 * ROWS
    strips = base.shape[0] // fine
    whole_copies = [
        pltpu.make_async_copy(source, dest, in_sems.at[strips + k])
        for k, (source, dest) in enumerate([(weights_hbm.at[kind], kernel), (pairs_hbm, pairs)])
    ]

    def rows(n):
        return pl.ds(n * fine, fine)

    base_copies = [
        pltpu.make_async_copy(base_hbm.at[rows(n)], base.at[rows(n)], in_sems.at[n])
        for n in range(strips)
    ]
    out_copies = [
        pltpu.make_async_copy(out.at[rows(n)], out_hbm.at[rows(n)], out_sems.at[n])
        for n in range(strips)
    ]
    for copy in whole_copies + base_copies:
        copy.start()
    for copy in whole_copies:
        copy.wait()

    def tap(row, col):
        k = 3 * row + col
        block = kernel[k * C : (k + 1) * C, :]
        return block.T if swapped else block

    def lanes(*pieces):
        return jnp.concatenate(pieces, axis=1)

    odd_kernel = jnp.concatenate([lanes(tap(1, 2), tap(2, 2)), lanes(tap(1, 0), tap(2, 0))], axis=0)
    last_kernel = jnp.concatenate([tap(0, 2), tap(0, 0)], axis=0)
    even_kernel = jnp.concatenate(
        [lanes(tap(1, 1), tap(2, 1)), lanes(jnp.zeros((C, C), BF16), tap(0, 1))], axis=0
    )
    for n in range(strips):
        at = ROWS * n + above
        near = flat(pairs[at : at + ROWS])
        far = flat(pairs[at + 1 : at + 1 + ROWS])
        odd = dot(near, odd_kernel)
        last = dot(far, last_kernel)
        even = dot(lanes(near[:, :C], far[:, :C]), even_kernel)
        for k in range(ROWS):
            at_k = slice(k * half_cols, (k + 1) * half_cols)
            whole[2 * k, pl.ds(0, half_cols, stride=2), :] = even[at_k, :C]
            whole[2 * k, pl.ds(1, half_cols, stride=2), :] = odd[at_k, :C]
            whole[2 * k + 1, pl.ds(0, half_cols, stride=2), :] = even[at_k, C:]
            whole[2 * k + 1, pl.ds(1, half_cols, stride=2), :] = odd[at_k, C:] + last[at_k]
        base_copies[n].wait()
        out[rows(n)] = (base[rows(n)].astype(F32) + whole[...]).astype(BF16)
        out_copies[n].start()
    for copy in out_copies:
        copy.wait()


def spread(name, above, kind, swapped, pairs, base, weights):
    rows, cols, _ = base.shape
    strips = rows // (2 * ROWS)
    hbm = pl.BlockSpec(memory_space=pltpu.HBM)
    return pl.pallas_call(
        functools.partial(up_kernel, above, kind, swapped),
        out_shape=jax.ShapeDtypeStruct(base.shape, BF16),
        in_specs=[hbm] * 3,
        out_specs=hbm,
        scratch_shapes=[
            pltpu.VMEM(shape, BF16)
            for shape in (pairs.shape, base.shape, weights.shape[1:], base.shape)
        ]
        + [
            pltpu.VMEM((2 * ROWS, cols, C), F32),
            pltpu.SemaphoreType.DMA((strips + 2,)),
            pltpu.SemaphoreType.DMA((strips,)),
        ],
        compiler_params=pltpu.CompilerParams(vmem_limit_bytes=60 * 2**20),
        cost_estimate=pl.CostEstimate(
            flops=9 * rows * cols * C * C // 2, transcendentals=0, bytes_accessed=7 * 2**20
        ),
        name=name,
    )(pairs, base, weights)


def copied(name, out_shapes, moves, limit, *arrays):
    def kernel(*refs):
        ins, outs, sems = refs[: len(arrays)], refs[len(arrays) : -1], refs[-1]
        copies = [
            pltpu.make_async_copy(ins[i].at[cut], outs[o].at[place], sems.at[k])
            for k, (i, cut, o, place) in enumerate(moves)
        ]
        for copy in copies:
            copy.start()
        for copy in copies:
            copy.wait()

    return pl.pallas_call(
        kernel,
        out_shape=tuple(jax.ShapeDtypeStruct(shape, BF16) for shape in out_shapes),
        in_specs=[pl.BlockSpec(memory_space=pl.ANY)] * len(arrays),
        out_specs=(pl.BlockSpec(memory_space=pltpu.VMEM),) * len(out_shapes),
        scratch_shapes=[pltpu.SemaphoreType.DMA((len(moves),))],
        compiler_params=pltpu.CompilerParams(vmem_limit_bytes=limit * 2**20),
        name=name,
    )(*arrays)


def pack_kernel(fields_hbm, cot_hbm, east, west, up, down, ends, spare, sems):
    rows, cols, _ = fields_hbm.shape
    column_copies = [
        pltpu.make_async_copy(source.at[:, pl.ds(at, 8), :], ends.at[k], sems.at[k])
        for k, (source, at) in enumerate(
            [(fields_hbm, cols - 8), (cot_hbm, cols - 8), (fields_hbm, 0), (cot_hbm, 0)]
        )
    ]
    row_copies = [
        pltpu.make_async_copy(
            source.at[pl.ds(at, count)], dest.at[pl.ds(place, count)], sems.at[4 + k]
        )
        for k, (source, at, count, dest, place) in enumerate(
            [
                (fields_hbm, rows - FIELD_LOW, FIELD_LOW, up, 0),
                (cot_hbm, rows - COT_LOW, COT_LOW, up, FIELD_LOW),
                (fields_hbm, 0, FIELD_HIGH, down, 0),
                (cot_hbm, 0, COT_HIGH, down, FIELD_HIGH),
            ]
        )
    ]
    for copy in column_copies + row_copies:
        copy.start()
    for copy in column_copies:
        copy.wait()
    field, other = ends[0].astype(F32), ends[1].astype(F32)
    east[...] = jnp.concatenate(
        [other[:, 8 - COT_LOW :], field[:, 8 - FIELD_LOW :]], axis=1
    ).astype(BF16)
    field, other = ends[2].astype(F32), ends[3].astype(F32)
    beside = 8 - FIELD_HIGH
    west[:rows] = jnp.concatenate([field[:, :FIELD_HIGH], other[:, :beside]], axis=1).astype(BF16)
    other = other.reshape(rows // 4, 4, 8, C)
    for k in range(4):
        spare[:, 2 * k : 2 * k + 2, :] = other[:, k, beside:COT_HIGH]
    west[rows:] = spare[...].astype(BF16)
    for copy in row_copies:
        copy.wait()


def packed(fields, cot):
    rows, cols, _ = fields.shape
    vmem = pl.BlockSpec(memory_space=pltpu.VMEM)
    return pl.pallas_call(
        pack_kernel,
        out_shape=(
            jax.ShapeDtypeStruct((rows, 8, C), BF16),
            jax.ShapeDtypeStruct((rows + rows // 4, 8, C), BF16),
            jax.ShapeDtypeStruct((FIELD_LOW + COT_LOW, cols, C), BF16),
            jax.ShapeDtypeStruct((FIELD_HIGH + COT_HIGH, cols, C), BF16),
        ),
        in_specs=[pl.BlockSpec(memory_space=pl.ANY)] * 2,
        out_specs=(vmem,) * 4,
        scratch_shapes=[
            pltpu.VMEM((4, rows, 8, C), BF16),
            pltpu.VMEM((rows // 4, 8, C), F32),
            pltpu.SemaphoreType.DMA((8,)),
        ],
        compiler_params=pltpu.CompilerParams(vmem_limit_bytes=52 * 2**20),
        name="pack",
    )(fields, cot)


def passed(*arrays):
    hbm = pl.BlockSpec(memory_space=pl.ANY)
    return pl.pallas_call(
        lambda *refs: None,
        out_shape=tuple(jax.ShapeDtypeStruct(array.shape, array.dtype) for array in arrays),
        in_specs=[hbm] * len(arrays),
        out_specs=(hbm,) * len(arrays),
        input_output_aliases={k: k for k in range(len(arrays))},
        compiler_params=pltpu.CompilerParams(vmem_limit_bytes=2**20),
        name="passed",
    )(*arrays)


def halos(fields, cot, weights):
    lat = lax.axis_size("lat")
    lon = lax.axis_size("lon")
    rows = fields.shape[0]
    every = slice(None)

    def row(start, count):
        return (pl.ds(start, count), every, every)

    east, west, up, down = packed(fields, cot)
    up, down = passed(up, down)
    north = [(i, i + 1) for i in range(lat - 1)]
    south = [(j, i) for i, j in north]
    eastward = [(i, (i + 1) % lon) for i in range(lon)]
    westward = [(j, i) for i, j in eastward]
    from_west = lax.ppermute(east, "lon", eastward)
    from_east = lax.ppermute(west, "lon", westward)
    low = lax.ppermute(up, "lat", north)
    high = lax.ppermute(down, "lat", south)
    spare = rows + (rows - FIELD_LOW) // 4
    up, down = copied(
        "corners",
        [(LOW_ENDS, 8, C), (HIGH_ENDS, 8, C)],
        [
            (0, row(rows - FIELD_LOW, FIELD_LOW), 0, row(0, FIELD_LOW)),
            (1, row(rows - FIELD_LOW, FIELD_LOW), 0, row(FIELD_LOW, FIELD_LOW)),
            (1, row(spare, 2), 0, row(2 * FIELD_LOW, 2)),
            (0, row(0, FIELD_HIGH), 1, row(0, FIELD_HIGH)),
            (1, row(0, FIELD_HIGH), 1, row(FIELD_HIGH, FIELD_HIGH)),
            (1, row(rows, 2), 1, row(2 * FIELD_HIGH, 2)),
        ],
        2,
        from_west,
        from_east,
    )
    up, down, weights = lax.optimization_barrier((up, down, weights))
    low_ends = lax.ppermute(up, "lat", north)
    high_ends = lax.ppermute(down, "lat", south)
    weights = lax.all_gather(weights, "dp", axis=3, tiled=True)
    return (low, high, from_west, from_east, low_ends, high_ends), weights


def body(fields, down_weight, mid_weight, up_weight, cotangent):
    lats, lons, parts = (lax.axis_size(axis) for axis in ("lat", "lon", "dp"))
    _, rows, cols, _ = fields.shape
    half_rows, half_cols = rows // 2, cols // 2
    scale = 1.0 / math.sqrt(parts * rows * lats * cols * lons)
    fields, cotangent = fields[0], cotangent[0]
    weights = jnp.stack([down_weight, mid_weight, up_weight])
    edges, weights = halos(fields, cotangent, weights)
    weights = weights.reshape(3, 9 * C, C)

    slots = half_cols + EDGE
    quads = half_rows // 2 + 5
    pairs = half_rows // 2 + 3
    hbm = pl.BlockSpec(memory_space=pl.ANY)
    inputs = (fields, cotangent, *edges, weights)
    own, other, mid_pairs, grad_pairs = pl.pallas_call(
        functools.partial(grads_kernel, half_rows, half_cols, lats, scale),
        out_shape=(
            jax.ShapeDtypeStruct((TAPS, C // 2, C), F32),
            jax.ShapeDtypeStruct((TAPS, C // 2, C), BF16),
            jax.ShapeDtypeStruct((pairs, 2, half_cols, 2 * C), BF16),
            jax.ShapeDtypeStruct((pairs, 2, half_cols, 2 * C), BF16),
        ),
        in_specs=[hbm] * len(inputs),
        out_specs=(pl.BlockSpec(memory_space=pltpu.VMEM),) * 2
        + (pl.BlockSpec(memory_space=pltpu.HBM),) * 2,
        scratch_shapes=[pltpu.VMEM(array.shape, BF16) for array in inputs]
        + [
            pltpu.VMEM((15 * C, 2 * C), BF16),
            pltpu.VMEM((12 * C, 2 * C), BF16),
            pltpu.VMEM((15 * C, 2 * C), BF16),
            pltpu.VMEM((12 * C, 2 * C), BF16),
            pltpu.VMEM((pairs, 2, half_cols, 2 * C), BF16),
            pltpu.VMEM((pairs, 2, half_cols, 2 * C), BF16),
            pltpu.VMEM((quads, 4, slots, 3 * C), BF16),
            pltpu.VMEM((quads, 4, slots, 3 * C), BF16),
            pltpu.VMEM((pairs + 1, 2, slots, 3 * C), BF16),
            pltpu.VMEM((pairs + 1, 2, slots, 3 * C), BF16),
            pltpu.VMEM((4, cols + 48, C), F32),
            pltpu.VMEM((PAIRS, slots + 16, C), F32),
            pltpu.VMEM((3, C, 9 * C), F32),
            pltpu.SemaphoreType.DMA((6,)),
            pltpu.SemaphoreType.DMA((2, CHUNKS)),
            pltpu.SemaphoreType.DMA,
            pltpu.SemaphoreType.DMA((2,)),
        ],
        compiler_params=pltpu.CompilerParams(vmem_limit_bytes=50 * 2**20),
        cost_estimate=pl.CostEstimate(
            flops=70 * 2 * half_rows * half_cols * C * C,
            transcendentals=half_rows * half_cols * C,
            bytes_accessed=8 * 2**20,
        ),
        name="grads",
    )(*inputs)
    mid_pairs = mid_pairs.reshape(2 * pairs, half_cols, 2 * C)
    grad_pairs = grad_pairs.reshape(2 * pairs, half_cols, 2 * C)

    came = lax.ppermute(other, "dp", [(0, 1), (1, 0)])
    both = (own + came.astype(F32)).astype(BF16)
    pieces = both.reshape(lats * lons, -1, C)
    pieces = lax.all_to_all(pieces, ("lat", "lon"), 0, 0, tiled=True)
    piece = jnp.sum(pieces.astype(F32), axis=0, keepdims=True).astype(BF16)
    totals = lax.all_to_all(
        jnp.broadcast_to(piece, pieces.shape), ("lat", "lon"), 0, 0, tiled=True
    )
    _, mid_pairs, grad_pairs = lax.optimization_barrier((piece, mid_pairs, grad_pairs))
    level_out = spread("level", 1, 2, False, mid_pairs, fields, weights)
    grad_fields = spread("gradient", 0, 0, True, grad_pairs, cotangent, weights)
    totals = totals.reshape(TAPS, C // 2, C).astype(F32)
    grad_down, grad_mid, grad_up = (
        totals[9 * k : 9 * k + 9].reshape(3, 3, C // 2, C) for k in range(3)
    )
    return (level_out[None], grad_fields[None], grad_down, grad_mid, grad_up)


def solution(mesh):
    field = P("dp", "lat", "lon", None)
    weight = P(None, None, "dp", None)
    return jax.shard_map(
        body,
        mesh=mesh,
        in_specs=(field, weight, weight, weight, field),
        out_specs=(field, field, weight, weight, weight),
        check_vma=False,
    )
```
